32 devices in a mesh: dp: 8 (over y, x, core), seq: 4 (over z).
Axes of the slice: x: 2, y: 2, z: 4, core: 2. Of those that a mesh axis runs over, the one named last changes fastest.
Arguments:
- tokens: bfloat16 [16, 1024, 768], P('dp', 'seq'), may hold values from -6 to 6
- lengths: int32 [16], P('dp'), may hold values from 128 to 1024, as said below
- head_swap: int32 [12], replicated, may hold values from 0 to 1, as said below
- w_qkv: bfloat16 [768, 2304], replicated, may hold values from -0.21875 to 0.21875
- bias_q: float32 [768], replicated, may hold values from -3 to 3
- bias_v: float32 [768], replicated, may hold values from -3 to 3
- w_out: bfloat16 [768, 768], replicated, may hold values from -2.5 to 2.5
- bias_out: float32 [768], replicated, may hold values from -3 to 3
- gain_attn: float32 [768], replicated, may hold values from 0.5 to 1.5
- shift_attn: float32 [768], replicated, may hold values from -3 to 3
- w_up: bfloat16 [768, 3072], replicated, may hold values from -0.21875 to 0.21875
- bias_up: float32 [3072], replicated, may hold values from -3 to 3
- w_down: bfloat16 [3072, 768], replicated, may hold values from -0.109375 to 0.109375
- bias_down: float32 [768], replicated, may hold values from -3 to 3
- gain_ffn: float32 [768], replicated, may hold values from 0.5 to 1.5
- shift_ffn: float32 [768], replicated, may hold values from -3 to 3
- cotangent: bfloat16 [16, 1024, 768], P('dp', 'seq'), may hold values from -6 to 6
Outputs:
- output: bfloat16 [16, 1024, 768], P('dp', 'seq')
- d_tokens: float32 [16, 1024, 768], P('dp', 'seq')
- g_w_qkv: float32 [768, 2304], P('seq')
- g_bias_q: float32 [768], P('seq')
- g_bias_v: float32 [768], P('seq')
- g_w_out: float32 [768, 768], P('seq')
- g_bias_out: float32 [768], P('seq')
- g_gain_attn: float32 [768], P('seq')
- g_shift_attn: float32 [768], P('seq')
- g_w_up: float32 [768, 3072], P('seq')
- g_bias_up: float32 [3072], P('seq')
- g_w_down: float32 [3072, 768], P('seq')
- g_bias_down: float32 [768], P('seq')
- g_gain_ffn: float32 [768], P('seq')
- g_shift_ffn: float32 [768], P('seq')
The draws below stay inside these ranges and needn't reach their ends.
Inputs may be any that keep to these rules, and one draw needn't show every extreme that they name: `lengths`: positions at or past a sequence's length are padding; some sequence has 1024 and some has 128. `head_swap`: 1 where a head's queries of each block use the other block's keys, 0 where they use their own block's; both occur.
All inputs are finite; a program needn't handle non-finite values.
Results may differ from the reference program's by a relative error of at most 0.014.
Values may be sent and summed in bfloat16 or wider, within the bound.
No kernel may reach another device: no remote copies, remote signals or barrier semaphores. Data moves between devices by JAX's collectives and lax.ppermute only.
A program may use at most 192 MiB of HBM per device.

```python
import math
import jax
import jax.numpy as jnp
from jax import lax

D = 768
HEADS = 12
HEAD_DIM = 64
FF = 3072
BLOCK = 512
MIN_LEN = 128
LENGTH = 1024
SEQS = 16


def draw_lengths(key, part):
    first, second, third = jax.random.split(key, 3)
    values = jax.random.randint(first, (SEQS,), MIN_LEN, LENGTH + 1)
    longest = jax.random.randint(second, (), 0, SEQS)
    shortest = (longest + 1 + jax.random.randint(third, (), 0, SEQS - 1)) % SEQS
    index = jnp.arange(SEQS)
    values = jnp.where(index == longest, LENGTH, values)
    values = jnp.where(index == shortest, MIN_LEN, values)
    return values.astype(jnp.int32)


def draw_head_swap(key, part):
    first, second, third = jax.random.split(key, 3)
    values = jax.random.randint(first, (HEADS,), 0, 2)
    keeper = jax.random.randint(second, (), 0, HEADS)
    mover = (keeper + 1 + jax.random.randint(third, (), 0, HEADS - 1)) % HEADS
    index = jnp.arange(HEADS)
    values = jnp.where(index == keeper, 0, values)
    values = jnp.where(index == mover, 1, values)
    return values.astype(jnp.int32)


def shard_levels(stream_key, dims, pieces, low, top_value):
    level = 1.0
    for dim, parts in pieces:
        steps = jax.random.uniform(jax.random.fold_in(jax.random.fold_in(stream_key, 6), dim), (parts,), jnp.float32, low / len(pieces), top_value / len(pieces))
        level = level * jnp.repeat(jnp.exp(steps), dims[dim] // parts).reshape((-1,) + (1,) * (len(dims) - 1 - dim))
    return level


def noise(own_key, shape, deviation, most, cuts=(), kind=jnp.bfloat16):
    factor_of = shard_levels(own_key, shape, cuts, -0.22, 0.18) if cuts else 1.0
    values = jax.random.normal(own_key, shape, jnp.float32) * deviation * factor_of
    return jnp.minimum(jnp.maximum(values, -most), most).astype(kind)


def setup_inputs(seed: int = 0) -> dict:
    key_of = jax.random.split(jax.random.key(seed), 18)
    tokens = noise(key_of[0], (SEQS, LENGTH, D), 1.0, 6.0, ((0, 8), (1, 4)))
    lengths = draw_lengths(jax.random.fold_in(key_of[17], 71), 0)
    head_swap = draw_head_swap(jax.random.fold_in(key_of[17], 71), 0)
    w_qkv = noise(key_of[3], (D, 3 * D), D ** -0.5, 0.21875)
    bias_q = noise(key_of[4], (D,), 0.5, 3.0, (), jnp.float32)
    bias_v = noise(key_of[5], (D,), 0.5, 3.0, (), jnp.float32)
    w_out = noise(key_of[6], (D, D), (max(D // 128, 1)) ** -0.5, 2.5)
    bias_out = noise(key_of[7], (D,), 0.5, 3.0, (), jnp.float32)
    gain_attn = jnp.clip(1.0 + 0.1 * jax.random.normal(key_of[8], (D,), jnp.float32), 0.5, 1.5)
    shift_attn = noise(key_of[9], (D,), 0.5, 3.0, (), jnp.float32)
    w_up = noise(key_of[10], (D, FF), D ** -0.5, 0.21875)
    bias_up = noise(key_of[11], (FF,), 0.5, 3.0, (), jnp.float32)
    w_down = noise(key_of[12], (FF, D), FF ** -0.5, 0.109375)
    bias_down = noise(key_of[13], (D,), 0.5, 3.0, (), jnp.float32)
    gain_ffn = jnp.clip(1.0 + 0.1 * jax.random.normal(key_of[14], (D,), jnp.float32), 0.5, 1.5)
    shift_ffn = noise(key_of[15], (D,), 0.5, 3.0, (), jnp.float32)
    cotangent = noise(key_of[16], (SEQS, LENGTH, D), 1.0, 6.0, ((0, 8), (1, 4)))
    return {"tokens": tokens, "lengths": lengths, "head_swap": head_swap, "w_qkv": w_qkv, "bias_q": bias_q, "bias_v": bias_v, "w_out": w_out, "bias_out": bias_out, "gain_attn": gain_attn, "shift_attn": shift_attn, "w_up": w_up, "bias_up": bias_up, "w_down": w_down, "bias_down": bias_down, "gain_ffn": gain_ffn, "shift_ffn": shift_ffn, "cotangent": cotangent}


@jax.custom_vjp
def low(v):
    return lax.optimization_barrier(v.astype(jnp.bfloat16)).astype(jnp.float32)

@jax.custom_vjp
def low_back(v):
    return v

def low_keep(v):
    return (low(v), None)

def low_pass(kept, grad):
    return (grad,)

def back_keep(v):
    return (v, None)

def back_low(kept, grad):
    return (low(grad),)
low.defvjp(low_keep, low_pass)
low_back.defvjp(back_keep, back_low)

def layer_norm(hidden, gain, shift):
    center = hidden - lax.optimization_barrier(jnp.mean(hidden, -1, keepdims=True))
    spread = lax.optimization_barrier(jnp.mean(center * center, -1, keepdims=True))
    return center * lax.rsqrt(spread + 1e-05) * gain + shift

def forward(params, inputs, valid, head_swap):
    w_qkv, bias_q, bias_v, w_out, bias_out, gain_attn, shift_attn, w_up, bias_up, w_down, bias_down, gain_ffn, shift_ffn = params
    highest = lax.Precision.HIGHEST
    count = inputs.shape[0]
    proj = jnp.einsum('gld,de->gle', inputs, w_qkv, precision=highest)
    query = low_back(low(proj[..., :D] + bias_q))
    keys = low_back(low(proj[..., D:2 * D]))
    values = low_back(low(proj[..., 2 * D:] + bias_v))
    swapped = head_swap == 1
    chosen = swapped[None, None, None, :, None]
    q_blocks = query.reshape(count, 2, BLOCK, HEADS, HEAD_DIM)
    k_blocks = keys.reshape(count, 2, BLOCK, HEADS, HEAD_DIM)
    v_blocks = values.reshape(count, 2, BLOCK, HEADS, HEAD_DIM)
    k_blocks = jnp.where(chosen, k_blocks[:, ::-1], k_blocks)
    v_blocks = jnp.where(chosen, v_blocks[:, ::-1], v_blocks)
    valid_blocks = valid.reshape(count, 2, BLOCK)
    key_ok = jnp.where(swapped[None, None, :, None], valid_blocks[:, ::-1][:, :, None, :], valid_blocks[:, :, None, :])
    raw = jnp.einsum('gbqhd,gbkhd->gbhqk', q_blocks, k_blocks, precision=highest) * HEAD_DIM ** (-0.5)
    raw = low_back(raw)
    masked = jnp.where(key_ok[:, :, :, None, :], raw, jnp.float32(-10000.0))
    probs = jax.nn.softmax(masked, axis=-1)
    context = jnp.einsum('gbhqk,gbkhd->gbqhd', low(probs), v_blocks, precision=highest)
    context = low_back(low(context)).reshape(count, LENGTH, D)
    attn = low_back(jnp.einsum('gld,de->gle', context, w_out, precision=highest) + bias_out)
    y_one = low(layer_norm(inputs + attn, gain_attn, shift_attn))
    pre = low_back(jnp.einsum('gld,df->glf', y_one, w_up, precision=highest) + bias_up)
    act = low(jax.nn.gelu(pre, approximate=False))
    ffn = low_back(jnp.einsum('glf,fd->gld', act, w_down, precision=highest) + bias_down)
    return layer_norm(y_one + ffn, gain_ffn, shift_ffn)

def reference(tokens, lengths, head_swap, w_qkv, bias_q, bias_v, w_out, bias_out, gain_attn, shift_attn, w_up, bias_up, w_down, bias_down, gain_ffn, shift_ffn, cotangent):
    params = tuple((item.astype(jnp.float32) for item in (w_qkv, bias_q, bias_v, w_out, bias_out, gain_attn, shift_attn, w_up, bias_up, w_down, bias_down, gain_ffn, shift_ffn)))
    group = math.gcd(SEQS, max(1, 4096 // LENGTH))
    steps_count = SEQS // group
    inputs = tokens.astype(jnp.float32).reshape(steps_count, group, LENGTH, D)
    grads_in = cotangent.astype(jnp.float32).reshape(steps_count, group, LENGTH, D)
    lens = lengths.astype(jnp.int32).reshape(steps_count, group)
    positions = jnp.arange(LENGTH, dtype=jnp.int32)

    def one_group(totals, item):
        block_in, block_grad, block_lens = item
        valid = positions[None, :] < block_lens[:, None]
        result, pull = jax.vjp(lambda p, x: forward(p, x, valid, head_swap), params, block_in)
        param_grads, input_grad = pull(block_grad)
        totals = tuple((a + b for a, b in zip(totals, param_grads)))
        return (totals, (result.astype(jnp.bfloat16), input_grad))
    start = tuple((jnp.zeros(item.shape, jnp.float32) for item in params))
    totals, (results, input_grads) = lax.scan(one_group, start, (inputs, grads_in, lens))
    return (results.reshape(SEQS, LENGTH, D), input_grads.reshape(SEQS, LENGTH, D), totals[0], totals[1], totals[2], totals[3], totals[4], totals[5], totals[6], totals[7], totals[8], totals[9], totals[10], totals[11], totals[12])
```

```python
import jax
import jax.numpy as jnp
from jax import lax
from jax.experimental import pallas as pl
from jax.experimental.pallas import tpu as pltpu
from jax.sharding import PartitionSpec as P

f32 = jnp.float32
bf16 = jnp.bfloat16
NN = (((1,), (0,)), ((), ()))
NT = (((1,), (1,)), ((), ()))


def mm(a, b, dims=NN):
    return lax.dot_general(a, b, dims, preferred_element_type=f32)


def shape(*dims, dtype=bf16):
    return jax.ShapeDtypeStruct(dims, dtype)


def whole(arr):
    zeros = (0,) * arr.ndim
    return pl.BlockSpec(arr.shape, lambda *_: zeros)


def call(kernel, name, grid, specs, outs, out_specs, scratch, scalars, *args):
    return pl.pallas_call(
        kernel,
        grid_spec=pltpu.PrefetchScalarGridSpec(
            num_scalar_prefetch=1,
            grid=grid,
            in_specs=specs,
            out_specs=out_specs,
            scratch_shapes=scratch,
        ),
        out_shape=outs,
        name=name,
    )(scalars, *args)


def limits(info, pair, h, place, half):
    swap = info[4 + 2 * pair + h]
    first = jnp.where(swap == 1, info[2], info[0])
    second = jnp.where(swap == 1, info[3], info[1])
    return place < jnp.where(place < half, first, second + half)


def attn_fwd_kernel(info, q_ref, k_ref, v_ref, ctx_ref, p_ref):
    pair = pl.program_id(0)
    rows, lanes = q_ref.shape
    hd = lanes // 2
    lane = lax.broadcasted_iota(jnp.int32, (rows, lanes), 1)
    place = lax.broadcasted_iota(jnp.int32, (rows, rows), 0)
    q = q_ref[...]
    k = k_ref[...]
    vt = jnp.transpose(v_ref[...])
    parts = []
    for h in range(2):
        mine = (lane < hd) if h == 0 else (lane >= hd)
        s = mm(jnp.where(mine, k, jnp.zeros_like(k)), q, NT)
        s = jnp.where(limits(info, pair, h, place, rows // 2), s, f32(-10000.0))
        e = jnp.exp(s - jnp.max(s, 0, keepdims=True))
        p = (e * (1.0 / jnp.sum(e, 0, keepdims=True))).astype(bf16)
        p_ref[h] = p
        parts.append(mm(vt[h * hd : (h + 1) * hd], p))
    ctx_ref[...] = jnp.transpose(jnp.concatenate(parts, 0)).astype(bf16)


def attn_fwd(info, q, k, v):
    rows, width = q.shape
    pairs = width // 128
    blk = pl.BlockSpec((rows, 128), lambda j, s: (0, j))
    sq = pl.BlockSpec((2, rows, rows), lambda j, s: (j, 0, 0))
    return call(
        attn_fwd_kernel, "attn_fwd", (pairs,), [blk] * 3,
        [shape(rows, width), shape(2 * pairs, rows, rows)], [blk, sq], [], info, q, k, v,
    )


def attn_bwd_kernel(info, q_ref, k_ref, v_ref, g_ref, p_ref, dq_ref, dk_ref, dv_ref):
    pair = pl.program_id(0)
    rows, lanes = q_ref.shape
    hd = lanes // 2
    lane = lax.broadcasted_iota(jnp.int32, (rows, lanes), 1)
    place = lax.broadcasted_iota(jnp.int32, (rows, lanes), 0)
    q = q_ref[...]
    k = k_ref[...]
    v = v_ref[...]
    g = g_ref[...]
    zero = jnp.zeros_like(k)
    oks = [limits(info, pair, h, place, rows // 2) for h in range(2)]
    ok = jnp.where(lane < hd, jnp.where(oks[0], 1, 0), jnp.where(oks[1], 1, 0)) == 1
    kt = jnp.transpose(jnp.where(ok, k, zero))
    dvs, dks, dqs = [], [], []
    for h in range(2):
        mine = (lane < hd) if h == 0 else (lane >= hd)
        dp = mm(jnp.where(mine, v, zero), g, NT)
        pb = p_ref[h]
        p = pb.astype(f32)
        inner = jnp.sum(p * dp, 0, keepdims=True)
        ds = (p * (dp - inner)).astype(bf16)
        dvs.append(mm(pb, g))
        dks.append(mm(ds, q))
        dqs.append(mm(kt[h * hd : (h + 1) * hd], ds))
    dv_ref[...] = jnp.where(lane < hd, dvs[0], dvs[1]).astype(bf16)
    dk_ref[...] = jnp.where(ok, jnp.where(lane < hd, dks[0], dks[1]), f32(0.0)).astype(bf16)
    dq_ref[...] = (jnp.transpose(jnp.concatenate(dqs, 0)) * f32(hd**-0.5)).astype(bf16)


def attn_bwd(info, q, k, v, g, p):
    rows, width = q.shape
    pairs = width // 128
    blk = pl.BlockSpec((rows, 128), lambda j, s: (0, j))
    sq = pl.BlockSpec((2, rows, rows), lambda j, s: (j, 0, 0))
    return call(
        attn_bwd_kernel, "attn_bwd", (pairs,), [blk] * 4 + [sq],
        [shape(rows, width)] * 3, [blk] * 3, [], info, q, k, v, g, p,
    )


def normalize(hidden):
    center = hidden - jnp.mean(hidden, -1, keepdims=True)
    rstd = lax.rsqrt(jnp.mean(center * center, -1, keepdims=True) + 1e-05)
    return center * rstd, rstd


def norm_back(scaled, normed, rstd):
    return rstd * (
        scaled
        - jnp.mean(scaled, -1, keepdims=True)
        - normed * jnp.mean(scaled * normed, -1, keepdims=True)
    )


def gelu_both(x):
    t = 1.0 / (1.0 + f32(0.3275911 * 0.7071067811865476) * jnp.abs(x))
    poly = f32(-1.453152027 / 2) + t * f32(1.061405429 / 2)
    poly = f32(1.421413741 / 2) + t * poly
    poly = f32(-0.284496736 / 2) + t * poly
    poly = t * (f32(0.254829592 / 2) + t * poly)
    bell = jnp.exp(x * x * f32(-0.5))
    tail = poly * bell
    dist = jnp.where(x >= 0, 1.0 - tail, tail)
    return x * dist, dist + x * bell * f32(0.3989422804014327)


def spans(me, width):
    half = width // 2
    mine = pl.multiple_of(me[0] * half, 128)
    theirs = pl.multiple_of((1 - me[0]) * half, 128)
    return pl.ds(mine, half), pl.ds(theirs, half)


def mid_one_kernel(
    me, x_ref, ctx_ref, wo_ref, bo_ref, gain_ref, shift_ref, wu_ref, bu_ref,
    y_ref, n_ref, r_ref, am_ref, at_ref, dm_ref, dt_ref, y_held,
):
    @pl.when(pl.program_id(0) == 0)
    def _():
        resid = x_ref[...].astype(f32) + (mm(ctx_ref[...], wo_ref[...]) + bo_ref[...])
        normed, rstd = normalize(resid)
        n_ref[...] = normed
        r_ref[...] = rstd
        y = (normed * gain_ref[...] + shift_ref[...]).astype(bf16)
        y_ref[...] = y
        y_held[...] = y

    for span, a_ref, d_ref in zip(spans(me, wu_ref.shape[1]), (am_ref, at_ref), (dm_ref, dt_ref)):
        pre = mm(y_held[...], wu_ref[:, span]) + bu_ref[:, span]
        act, slope = gelu_both(pre)
        a_ref[...] = act.astype(bf16)
        d_ref[...] = slope.astype(bf16)


def mid_one(me, x, ctx, wo, bo, gain, shift, wu, bu):
    rows, width = x.shape
    ff = wu.shape[1]
    parts = 4
    cut = ff // parts
    full = pl.BlockSpec((rows, width), lambda j, s: (0, 0))
    col = pl.BlockSpec((rows, cut // 2), lambda j, s: (0, j))
    return call(
        mid_one_kernel, "mid_one", (parts,),
        [full, full, whole(wo), whole(bo), whole(gain), whole(shift),
         pl.BlockSpec((width, cut), lambda j, s: (0, j)), pl.BlockSpec((1, cut), lambda j, s: (0, j))],
        [shape(rows, width), shape(rows, width, dtype=f32), shape(rows, 1, dtype=f32)]
        + [shape(rows, ff // 2)] * 4,
        [full, full, pl.BlockSpec((rows, 1), lambda j, s: (0, 0))] + [col] * 4,
        [pltpu.VMEM((rows, width), bf16)],
        me, x, ctx, wo, bo, gain, shift, wu, bu,
    )


def mid_two_kernel(
    me, am_ref, at_ref, wd_ref, bd_ref, y_ref, gain_ref, shift_ref, g_ref,
    out_ref, dtwo_ref, dffn_ref, vec_ref, acc,
):
    j = pl.program_id(0)
    mine, theirs = spans(me, wd_ref.shape[0])
    part = mm(am_ref[...], wd_ref[mine, :]) + mm(at_ref[...], wd_ref[theirs, :])

    @pl.when(j == 0)
    def _():
        acc[...] = part

    @pl.when(j > 0)
    def _():
        acc[...] += part

    @pl.when(j == pl.num_programs(0) - 1)
    def _():
        normed, rstd = normalize(y_ref[...].astype(f32) + (acc[...] + bd_ref[...]))
        out_ref[...] = (normed * gain_ref[...] + shift_ref[...]).astype(bf16)
        g = g_ref[...].astype(f32)
        d_two = norm_back(g * gain_ref[...], normed, rstd)
        dtwo_ref[...] = d_two
        d_ffn = d_two.astype(bf16)
        dffn_ref[...] = d_ffn
        vec_ref[0:1] = jnp.sum(g * normed, 0, keepdims=True)
        vec_ref[1:2] = jnp.sum(g, 0, keepdims=True)
        vec_ref[2:3] = jnp.sum(d_ffn.astype(f32), 0, keepdims=True)


def mid_two(me, am, at, wd, bd, y, gain, shift, g):
    rows, width = y.shape
    ff = wd.shape[0]
    parts = 4
    cut = ff // parts
    full = pl.BlockSpec((rows, width), lambda j, s: (0, 0))
    col = pl.BlockSpec((rows, cut // 2), lambda j, s: (0, j))
    return call(
        mid_two_kernel, "mid_two", (parts,),
        [col, col, pl.BlockSpec((cut, width), lambda j, s: (j, 0)), whole(bd), full, whole(gain),
         whole(shift), full],
        [shape(rows, width), shape(rows, width, dtype=f32), shape(rows, width),
         shape(3, width, dtype=f32)],
        [full, full, full, pl.BlockSpec((3, width), lambda j, s: (0, 0))],
        [pltpu.VMEM((rows, width), f32)],
        me, am, at, wd, bd, y, gain, shift, g,
    )


def back_one_kernel(me, dffn_ref, wd_ref, dm_ref, dt_ref, pm_ref, pt_ref, vec_ref):
    for span, d_ref, p_ref in zip(spans(me, wd_ref.shape[0]), (dm_ref, dt_ref), (pm_ref, pt_ref)):
        d_pre = (mm(dffn_ref[...], wd_ref[span, :], NT) * d_ref[...].astype(f32)).astype(bf16)
        p_ref[...] = d_pre
        vec_ref[:, span] = jnp.sum(d_pre.astype(f32), 0, keepdims=True)


def back_one(me, dffn, wd, dm, dt):
    rows, width = dffn.shape
    ff = wd.shape[0]
    parts = 4
    cut = ff // parts
    full = pl.BlockSpec((rows, width), lambda j, s: (0, 0))
    col = pl.BlockSpec((rows, cut // 2), lambda j, s: (0, j))
    return call(
        back_one_kernel, "back_one", (parts,),
        [full, pl.BlockSpec((cut, width), lambda j, s: (j, 0)), col, col],
        [shape(rows, ff // 2), shape(rows, ff // 2), shape(1, ff, dtype=f32)],
        [col, col, pl.BlockSpec((1, cut), lambda j, s: (0, j))],
        [], me, dffn, wd, dm, dt,
    )


def back_two_kernel(
    me, pm_ref, pt_ref, wu_ref, dtwo_ref, n_ref, r_ref, gain_ref, wo_ref,
    done_ref, dattn_ref, dctx_ref, vec_ref, acc,
):
    j = pl.program_id(0)
    mine, theirs = spans(me, wu_ref.shape[1])
    part = mm(pm_ref[...], wu_ref[:, mine], NT) + mm(pt_ref[...], wu_ref[:, theirs], NT)

    @pl.when(j == 0)
    def _():
        acc[...] = part

    @pl.when(j > 0)
    def _():
        acc[...] += part

    @pl.when(j == pl.num_programs(0) - 1)
    def _():
        d_y = acc[...] + dtwo_ref[...]
        normed = n_ref[...]
        d_one = norm_back(d_y * gain_ref[...], normed, r_ref[...])
        done_ref[...] = d_one
        d_attn = d_one.astype(bf16)
        dattn_ref[...] = d_attn
        dctx_ref[...] = mm(d_attn, wo_ref[...], NT).astype(bf16)
        vec_ref[0:1] = jnp.sum(d_y * normed, 0, keepdims=True)
        vec_ref[1:2] = jnp.sum(d_y, 0, keepdims=True)
        vec_ref[2:3] = jnp.sum(d_attn.astype(f32), 0, keepdims=True)


def back_two(me, pm, pt, wu, dtwo, n, r, gain, wo):
    rows, width = dtwo.shape
    ff = wu.shape[1]
    parts = 4
    cut = ff // parts
    full = pl.BlockSpec((rows, width), lambda j, s: (0, 0))
    col = pl.BlockSpec((rows, cut // 2), lambda j, s: (0, j))
    return call(
        back_two_kernel, "back_two", (parts,),
        [col, col, pl.BlockSpec((width, cut), lambda j, s: (0, j)), full, full, whole(r), whole(gain),
         whole(wo)],
        [shape(rows, width, dtype=f32), shape(rows, width), shape(rows, width),
         shape(3, width, dtype=f32)],
        [full, full, full, pl.BlockSpec((3, width), lambda j, s: (0, 0))],
        [pltpu.VMEM((rows, width), f32)],
        me, pm, pt, wu, dtwo, n, r, gain, wo,
    )


def put(tile, me, step, unit, group_rows, refs, column):
    a_keep, a_send, b_keep, b_send = refs
    for xr in range(2):
        for yr in range(2):
            for zr in range(4):
                slot = (zr & 1) * 2 + (zr >> 1)
                start = step(zr ^ me[3], 2 * (xr ^ me[1]) + (yr ^ me[2]))
                start = pl.multiple_of(start, unit)
                yield xr, yr, slot, start


def grad_down_kernel(me, lo_ref, lp_ref, ro_ref, rp_ref, ak, asd, bk, bsd, left, tile):
    rows = lo_ref.shape[0]

    @pl.when(pl.program_id(0) == 0)
    def _():
        left[:, :rows] = jnp.transpose(lo_ref[...])
        left[:, rows:] = jnp.transpose(lp_ref[...])

    tile[...] = mm(left[:, :rows], ro_ref[...]) + mm(left[:, rows:], rp_ref[...])
    depth = tile.shape[0] // 4
    size = depth // 2
    for xr in range(2):
        for yr in range(2):
            at = pl.multiple_of((2 * (xr ^ me[1]) + (yr ^ me[2])) * depth, size)
            (asd if xr else ak)[yr, 0] = tile[pl.ds(at, size), :].astype(bf16)
            at = pl.multiple_of(at + size, size)
            (bsd if yr else bk)[xr, 0] = tile[pl.ds(at, size), :].astype(bf16)


def grad_down(me, lo, lp, ro, rp):
    rows, width = lo.shape
    cut = ro.shape[1] // 4
    size = width // 8
    full = pl.BlockSpec((rows, width), lambda j, s: (0, 0))
    col = pl.BlockSpec((rows, cut), lambda j, s: (0, ((j >> 1) | ((j & 1) << 1)) ^ s[3]))
    out = pl.BlockSpec((2, 1, size, cut), lambda j, s: (0, j, 0, 0))
    return call(
        grad_down_kernel, "grad_down", (4,), [full, full, col, col],
        [shape(2, 4, size, cut)] * 4, [out] * 4,
        [pltpu.VMEM((width, 2 * rows), bf16), pltpu.VMEM((width, cut), f32)],
        me, lo, lp, ro, rp,
    )


def grad_up_kernel(me, lo_ref, lp_ref, ro_ref, rp_ref, ak, asd, bk, bsd, left, tile):
    rows = lo_ref.shape[0]
    j = pl.program_id(0)

    @pl.when(j == 0)
    def _():
        left[:, :rows] = jnp.transpose(lo_ref[...])
        left[:, rows:] = jnp.transpose(lp_ref[...])

    tile[...] = mm(left[:, :rows], ro_ref[...]) + mm(left[:, rows:], rp_ref[...])
    depth = tile.shape[0] // 4
    size = depth // 2

    def store(ref, offset):
        for zr in range(4):
            at = pl.multiple_of((zr ^ me[3]) * depth + offset, size)
            ref[0, (zr & 1) * 2 + (zr >> 1)] = tile[pl.ds(at, size), :].astype(bf16)

    for keep, send, bit, offset in ((ak, asd, j >> 1, 0), (bk, bsd, j & 1, size)):
        pl.when(bit == 0)(lambda: store(keep, offset))
        pl.when(bit == 1)(lambda: store(send, offset))


def grad_up(me, lo, lp, ro, rp):
    rows, width = lo.shape
    cut = ro.shape[1] // 4
    size = width // 8
    full = pl.BlockSpec((rows, width), lambda j, s: (0, 0))
    col = pl.BlockSpec((rows, cut), lambda j, s: (0, j ^ (2 * s[1] + s[2])))

    def out(index):
        return pl.BlockSpec((1, 4, size, cut), lambda j, s: (index(j), 0, 0, 0))

    return call(
        grad_up_kernel, "grad_up", (4,), [full, full, col, col],
        [shape(2, 4, size, cut)] * 4,
        [out(lambda j: jnp.minimum(j, 1)), out(lambda j: jnp.maximum(j - 2, 0)),
         out(lambda j: j >> 1), out(lambda j: j >> 1)],
        [pltpu.VMEM((width, 2 * rows), bf16), pltpu.VMEM((width, cut), f32)],
        me, lo, lp, ro, rp,
    )


def grad_rest_kernel(
    me, xo_ref, xp_ref, co_ref, cp_ref, qo_ref, qp_ref, ku_ref, kr_ref, vu_ref, vr_ref, ao_ref,
    ap_ref, far_ref, ak, asd, bk, bsd, left, tile,
):
    rows = xo_ref.shape[0]
    half = qp_ref.shape[1]
    mine = pl.ds(pl.multiple_of(me[0] * half, 128), half)
    far = far_ref[:, mine] == 1
    left[:, :rows] = jnp.transpose(xo_ref[...])
    left[:, rows:] = jnp.transpose(xp_ref[...])
    deep = tile.shape[0] // 4
    size = deep // 4
    for t in range(4):
        if t == 0:
            own, other = qo_ref[:, mine], qp_ref[...]
        elif t < 3:
            used, got = ((ku_ref, kr_ref), (vu_ref, vr_ref))[t - 1]
            used, got = used[:, mine], got[:, mine]
            own, other = jnp.where(far, got, used), jnp.where(far, used, got)
        else:
            left[:, :rows] = jnp.transpose(co_ref[...])
            left[:, rows:] = jnp.transpose(cp_ref[...])
            own, other = ao_ref[:, mine], ap_ref[...]
        tile[...] = mm(left[:, :rows], own) + mm(left[:, rows:], other)
        cols = slice((t % 2) * half, (t % 2 + 1) * half)
        for xr in range(2):
            for yr in range(2):
                for zr in range(4):
                    at = (zr ^ me[3]) * deep + (2 * (xr ^ me[1]) + (yr ^ me[2])) * size
                    piece = tile[pl.ds(pl.multiple_of(at, size), size), :].astype(bf16)
                    slot = (zr & 1) * 2 + (zr >> 1)
                    if t < 2:
                        (asd if xr else ak)[yr, slot, :, cols] = piece
                    else:
                        (bsd if yr else bk)[xr, slot, :, cols] = piece


def grad_rest(me, *args):
    rows, width = args[0].shape
    half = width // 2
    size = width // 16
    return call(
        grad_rest_kernel, "grad_rest", (1,), [whole(a) for a in args],
        [shape(2, 4, size, width)] * 4,
        [pl.BlockSpec((2, 4, size, width), lambda j, s: (0, 0, 0, 0))] * 4,
        [pltpu.VMEM((width, 2 * rows), bf16), pltpu.VMEM((width, half), f32)],
        me, *args,
    )


def local(
    dp, seq, tokens, lengths, head_swap, w_qkv, bias_q, bias_v, w_out, bias_out, gain_attn,
    shift_attn, w_up, bias_up, w_down, bias_down, gain_ffn, shift_ffn, cotangent,
):
    seqs_here, part_len, width = tokens.shape
    heads = head_swap.shape[0]
    head_dim = width // heads
    rows = seqs_here * part_len
    assert seqs_here == 2 and seq == 4 and dp % 8 == 0
    place = lax.axis_index("dp")
    z = lax.axis_index("seq")
    core, xbit, ybit = place & 1, (place >> 1) & 1, (place >> 2) & 1
    odd = z & 1
    me = jnp.stack([core, xbit, ybit, z]).astype(jnp.int32)

    def over_dp(arr, bit):
        return lax.ppermute(arr, "dp", [(i, i ^ bit) for i in range(dp)])

    def over_seq(arr, bit):
        return lax.ppermute(arr, "seq", [(i, i ^ bit) for i in range(seq)])

    def other(arr):
        return over_dp(arr, 1)

    def there(i, r):
        d, k = divmod(i, seq)
        return ((d & ~1) | (k >> 1)) * seq + 2 * (d & 1) + (r ^ (k & 1))

    ways = [[(i, there(i, r)) for i in range(dp * seq)] for r in range(2)]

    def gather_block(arr):
        return jnp.concatenate(
            [
                lax.ppermute(lax.dynamic_index_in_dim(arr, r ^ odd, 0, False), ("dp", "seq"), ways[r])
                for r in range(2)
            ],
            0,
        )

    def return_block(arr):
        back = [
            lax.ppermute(
                arr[r * part_len : (r + 1) * part_len], ("dp", "seq"), [(b, a) for a, b in ways[r]]
            )
            for r in range(2)
        ]
        return jnp.where(odd == 1, jnp.stack(back[::-1]), jnp.stack(back))

    x = gather_block(tokens)
    length = lax.ppermute(
        lax.dynamic_slice_in_dim(lengths, odd, 1, 0), ("dp", "seq"), ways[0]
    )[0]
    x_far = other(x)
    grad = gather_block(cotangent)

    def limit(block, half):
        return length - (block * rows + (half ^ odd) * part_len)

    info = jnp.concatenate(
        [
            jnp.stack([limit(core, 0), limit(core, 1), limit(1 - core, 0), limit(1 - core, 1)]),
            head_swap,
        ]
    ).astype(jnp.int32)
    far_lane = jnp.repeat(head_swap, head_dim)[None, :]
    far = far_lane == 1

    q = (mm(x, w_qkv[:, :width]) + bias_q).astype(bf16) * bf16(head_dim**-0.5)
    w_k, w_v = w_qkv[:, width : 2 * width], w_qkv[:, 2 * width :]
    k = jnp.where(far, mm(x_far, w_k), mm(x, w_k)).astype(bf16)
    v = (jnp.where(far, mm(x_far, w_v), mm(x, w_v)) + bias_v).astype(bf16)
    ctx, probs = attn_fwd(info, q, k, v)
    ctx_far = other(ctx)
    y, normed, rstd, act_m, act_t, slope_m, slope_t = mid_one(
        me, x, ctx, w_out, bias_out[None], gain_attn[None], shift_attn[None], w_up, bias_up[None]
    )
    y_far = other(y)
    act_far = other(act_t)
    out, d_two, d_ffn, vec_two = mid_two(
        me, act_m, act_t, w_down, bias_down[None], y, gain_ffn[None], shift_ffn[None], grad
    )
    output = return_block(out)

    d_ffn_far = other(d_ffn)
    pre_m, pre_t, vec_up = back_one(me, d_ffn, w_down, slope_m, slope_t)
    pre_far = other(pre_t)
    g_down = grad_down(me, d_ffn, d_ffn_far, act_m, act_far)
    d_one, d_attn, d_ctx, vec_one = back_two(
        me, pre_m, pre_t, w_up, d_two, normed, rstd, gain_attn[None], w_out
    )
    half = width // 2
    attn_far = other(lax.dynamic_slice_in_dim(d_attn, (1 - core) * half, half, 1))
    g_up = grad_up(me, y, y_far, pre_m, pre_far)
    d_q, d_ku, d_vu = attn_bwd(info, q, k, v, d_ctx, probs)
    d_kr, d_vr = other(d_ku), other(d_vu)
    q_far = other(lax.dynamic_slice_in_dim(d_q, (1 - core) * half, half, 1))
    g_rest = grad_rest(
        me, x, x_far, ctx, ctx_far, d_q, q_far, d_ku, d_kr, d_vu, d_vr, d_attn, attn_far,
        far_lane.astype(jnp.int32),
    )
    d_k = jnp.where(far, d_kr, d_ku)
    d_v = jnp.where(far, d_vr, d_vu)
    d_tok = mm(d_q, w_qkv[:, :width], NT) + mm(d_k, w_k, NT) + mm(d_v, w_v, NT) + d_one
    d_tokens = return_block(d_tok.astype(bf16)).astype(f32)

    def add(a, b):
        return (a.astype(f32) + b.astype(f32)).astype(bf16)

    def reduce(stored):
        a_keep, a_send, b_keep, b_send = stored
        a = add(a_keep, over_dp(a_send, 2))
        b = add(b_keep, over_dp(b_send, 4))
        a, b = add(a[0], over_dp(a[1], 4)), add(b[0], over_dp(b[1], 2))
        c = jnp.stack([a, b], 1)
        c = add(c[:2], over_seq(c[2:], 1))
        c = add(c[0], over_seq(c[1], 2))
        bit = 8
        while bit < dp:
            c = add(c, over_dp(c, bit))
            bit *= 2
        c = jnp.stack([c, over_dp(c, 4)])
        c = jnp.stack([c, over_dp(c, 2)])
        c = jnp.stack([c, other(c)])
        for axis, bit in enumerate((core, xbit, ybit)):
            c = jnp.where(bit == 1, jnp.flip(c, axis), c)
        return c.astype(f32)

    down = reduce(g_down)
    up = reduce(g_up)
    rest = reduce(g_rest)
    s_down = jnp.transpose(down, (0, 5, 1, 2, 3, 4)).reshape(-1, width)
    s_up = jnp.transpose(up, (3, 4, 1, 2, 0, 5)).reshape(width // seq, -1)
    rest = rest.reshape(2, 2, 2, 2, -1, 2, half)
    rest = jnp.transpose(rest, (3, 5, 1, 2, 4, 0, 6)).reshape(4, width // seq, width)
    s_qkv = jnp.concatenate([rest[0], rest[1], rest[2]], 1)
    s_out = rest[3]

    vec = jnp.concatenate(
        [
            jnp.sum(d_q, 0, dtype=f32), jnp.sum(d_v, 0, dtype=f32), vec_one.reshape(-1),
            vec_two.reshape(-1), vec_up.reshape(-1),
        ]
    ).reshape(-1, 128)
    bit = 1
    while bit < dp:
        vec = vec + over_dp(vec, bit)
        bit *= 2
    vec = vec + over_seq(vec, 1)
    vec = vec + over_seq(vec, 2)
    vec = vec.reshape(-1)
    wide = vec[: 8 * width].reshape(8, width)
    share = lax.dynamic_slice_in_dim(wide, z * (width // seq), width // seq, 1)
    tall = vec[8 * width :]
    s_b_up = lax.dynamic_slice_in_dim(tall, z * (tall.shape[0] // seq), tall.shape[0] // seq, 0)
    s_bq, s_bv, s_ga, s_sa, s_bo, s_gf, s_sf, s_bd = [share[i] for i in range(8)]
    return (
        output, d_tokens, s_qkv, s_bq, s_bv, s_out, s_bo, s_ga, s_sa, s_up, s_b_up, s_down, s_bd,
        s_gf, s_sf,
    )


def solution(mesh):
    dp, seq = mesh.shape["dp"], mesh.shape["seq"]
    rows = P("dp", "seq", None)
    placed = (rows, P("dp")) + (P(),) * 14 + (rows,)
    cut, line = P("seq", None), P("seq")
    return jax.shard_map(
        lambda *args: local(dp, seq, *args),
        mesh=mesh,
        in_specs=placed,
        out_specs=(
            rows, rows, cut, line, line, cut, line, line, line, cut, line, cut, line, line, line,
        ),
        check_vma=False,
    )
```

```python
import functools

import jax
import jax.numpy as jnp
from jax import lax
from jax.experimental import pallas as pl
from jax.experimental.pallas import tpu as pltpu
from jax.sharding import PartitionSpec as P


f32 = jnp.float32
bf16 = jnp.bfloat16
NN = (((1,), (0,)), ((), ()))
NT = (((1,), (1,)), ((), ()))


def mm(a, b, dims=NN):
    return lax.dot_general(a, b, dims, preferred_element_type=f32)


def shape(*dims, dtype=bf16):
    return jax.ShapeDtypeStruct(dims, dtype)


def whole(arr):
    zeros = (0,) * arr.ndim
    return pl.BlockSpec(arr.shape, lambda *_: zeros)


def call(kernel, grid, specs, outs, out_specs, scratch, scalars, *args, micros=8, mib=16):
    return pl.pallas_call(
        kernel,
        grid_spec=pltpu.PrefetchScalarGridSpec(
            num_scalar_prefetch=1,
            grid=grid,
            in_specs=specs,
            out_specs=out_specs,
            scratch_shapes=scratch,
        ),
        out_shape=outs,
        cost_estimate=pl.CostEstimate(
            flops=micros * 1_000_000_000, bytes_accessed=8_000_000, transcendentals=0
        ),
        compiler_params=pltpu.CompilerParams(vmem_limit_bytes=mib << 20),
    )(scalars, *args)


def limits(info, pair, h, place, half):
    swap = info[4 + 2 * pair + h]
    first = jnp.where(swap == 1, info[2], info[0])
    second = jnp.where(swap == 1, info[3], info[1])
    return place < jnp.where(place < half, first, second + half)


def attn_fwd_kernel(info, q_ref, k_ref, v_ref, ctx_ref, p_ref):
    pair = pl.program_id(0)
    rows, lanes = q_ref.shape
    hd = lanes // 2
    lane = lax.broadcasted_iota(jnp.int32, (rows, lanes), 1)
    place = lax.broadcasted_iota(jnp.int32, (rows, rows), 0)
    q = q_ref[...]
    k = k_ref[...]
    vt = jnp.transpose(v_ref[...])
    parts = []
    for h in range(2):
        mine = (lane < hd) if h == 0 else (lane >= hd)
        s = mm(jnp.where(mine, k, jnp.zeros_like(k)), q, NT)
        s = jnp.where(limits(info, pair, h, place, rows // 2), s, f32(-10000.0))
        e = jnp.exp(s - jnp.max(s, 0, keepdims=True))
        p = (e * (1.0 / jnp.sum(e, 0, keepdims=True))).astype(bf16)
        p_ref[h] = p
        parts.append(mm(vt[h * hd : (h + 1) * hd], p))
    ctx_ref[...] = jnp.transpose(jnp.concatenate(parts, 0)).astype(bf16)


def attn_fwd(info, q, k, v):
    rows, width = q.shape
    pairs = width // 128
    blk = pl.BlockSpec((rows, 128), lambda j, s: (0, j))
    sq = pl.BlockSpec((2, rows, rows), lambda j, s: (j, 0, 0))
    return call(
        attn_fwd_kernel, (pairs,), [blk] * 3,
        [shape(rows, width), pltpu.HBM((2 * pairs, rows, rows), bf16)], [blk, sq], [], info, q, k, v,
    )


def attn_bwd_kernel(
    start, info, q_ref, k_ref, v_ref, g_ref, p_ref, dq_ref, dk_ref, dv_ref, vec_ref
):
    pair = pl.program_id(0) + start
    rows, lanes = q_ref.shape
    hd = lanes // 2
    lane = lax.broadcasted_iota(jnp.int32, (rows, lanes), 1)
    place = lax.broadcasted_iota(jnp.int32, (rows, lanes), 0)
    q = q_ref[...]
    k = k_ref[...]
    v = v_ref[...]
    g = g_ref[...]
    zero = jnp.zeros_like(k)
    oks = [limits(info, pair, h, place, rows // 2) for h in range(2)]
    ok = jnp.where(lane < hd, jnp.where(oks[0], 1, 0), jnp.where(oks[1], 1, 0)) == 1
    kt = jnp.transpose(jnp.where(ok, k, zero))
    dvs, dks, dqs = [], [], []
    for h in range(2):
        mine = (lane < hd) if h == 0 else (lane >= hd)
        dp = mm(jnp.where(mine, v, zero), g, NT)
        pb = p_ref[h]
        p = pb.astype(f32)
        inner = jnp.sum(p * dp, 0, keepdims=True)
        ds = (p * (dp - inner)).astype(bf16)
        dvs.append(mm(pb, g))
        dks.append(mm(ds, q))
        dqs.append(mm(kt[h * hd : (h + 1) * hd], ds))
    dv = jnp.where(lane < hd, dvs[0], dvs[1]).astype(bf16)
    dq = (jnp.transpose(jnp.concatenate(dqs, 0)) * f32(hd**-0.5)).astype(bf16)
    dv_ref[...] = dv
    dk_ref[...] = jnp.where(ok, jnp.where(lane < hd, dks[0], dks[1]), f32(0.0)).astype(bf16)
    dq_ref[...] = dq
    vec_ref[0:1] = jnp.sum(dq.astype(f32), 0, keepdims=True)
    vec_ref[1:2] = jnp.sum(dv.astype(f32), 0, keepdims=True)


def attn_bwd(info, first, pairs, q, k, v, g, p):
    rows = q.shape[0]
    blk = pl.BlockSpec((rows, 128), lambda j, s: (0, j + first))
    sq = pl.BlockSpec((2, rows, rows), lambda j, s: (j + first, 0, 0))
    out = pl.BlockSpec((rows, 128), lambda j, s: (0, j))
    return call(
        functools.partial(attn_bwd_kernel, first), (pairs,), [blk] * 4 + [sq],
        [shape(rows, 128 * pairs)] * 3 + [shape(2, 128 * pairs, dtype=f32)],
        [out] * 3 + [pl.BlockSpec((2, 128), lambda j, s: (0, j))],
        [], info, q, k, v, g, p, micros=6, mib=16,
    )


def normalize(hidden):
    center = hidden - jnp.mean(hidden, -1, keepdims=True)
    rstd = lax.rsqrt(jnp.mean(center * center, -1, keepdims=True) + 1e-05)
    return center * rstd, rstd


def norm_back(scaled, normed, rstd):
    return rstd * (
        scaled
        - jnp.mean(scaled, -1, keepdims=True)
        - normed * jnp.mean(scaled * normed, -1, keepdims=True)
    )


def gelu_both(x):
    t = 1.0 / (1.0 + f32(0.3275911 * 0.7071067811865476) * jnp.abs(x))
    poly = f32(-1.453152027 / 2) + t * f32(1.061405429 / 2)
    poly = f32(1.421413741 / 2) + t * poly
    poly = f32(-0.284496736 / 2) + t * poly
    poly = t * (f32(0.254829592 / 2) + t * poly)
    bell = jnp.exp(x * x * f32(-0.5))
    tail = poly * bell
    dist = jnp.where(x >= 0, 1.0 - tail, tail)
    return x * dist, dist + x * bell * f32(0.3989422804014327)


def quarters(array, axis, cut):
    specs = []
    for far in range(2):
        for k in range(2):
            def index(j, s, far=far, k=k):
                at = 2 * (2 * j + k) + (s[0] ^ far)
                return (at, 0) if axis == 0 else (0, at)

            dims = list(array.shape)
            dims[axis] = cut
            specs.append(pl.BlockSpec(tuple(dims), index))
    return specs


def mid_kernel(
    me, x_ref, ctx_ref, wo_ref, bo_ref, ga_ref, sa_ref, wu0, wu1, wu2, wu3, bu0, bu1, bu2, bu3,
    wd0, wd1, wd2, wd3, bd_ref, gf_ref, sf_ref, g0_ref, g1_ref,
    y_ref, n_ref, r_ref, am_ref, at_ref, dm_ref, dt_ref, out_ref, dtwo_ref, dffn_ref, vec_ref,
    acc,
):
    j = pl.program_id(0)
    rows = x_ref.shape[0]
    part_len = rows // 2

    @pl.when(j == 0)
    def _():
        resid = x_ref[...].astype(f32) + (mm(ctx_ref[...], wo_ref[...]) + bo_ref[...])
        normed, rstd = normalize(resid)
        n_ref[...] = normed
        r_ref[...] = rstd
        y_ref[...] = (normed * ga_ref[...] + sa_ref[...]).astype(bf16)

    y = y_ref[...]
    part = None
    for wus, bus, wds, a_ref, d_ref in (
        ((wu0, wu1), (bu0, bu1), (wd0, wd1), am_ref, dm_ref),
        ((wu2, wu3), (bu2, bu3), (wd2, wd3), at_ref, dt_ref),
    ):
        up = jnp.concatenate([w[...] for w in wus], 1)
        pre = mm(y, up) + jnp.concatenate([b[...] for b in bus], 1)
        act, slope = gelu_both(pre)
        act = act.astype(bf16)
        a_ref[...] = act
        d_ref[...] = slope.astype(bf16)
        more = mm(act, jnp.concatenate([w[...] for w in wds], 0))
        part = more if part is None else part + more

    @pl.when(j == 0)
    def _():
        acc[...] = part

    @pl.when(j == 1)
    def _():
        acc[...] += part
        vec_ref[...] = jnp.zeros_like(vec_ref)
        for i, g_ref in enumerate((g0_ref, g1_ref)):
            at = slice(i * part_len, (i + 1) * part_len)
            normed, rstd = normalize(y_ref[at].astype(f32) + (acc[at] + bd_ref[...]))
            out_ref[at] = (normed * gf_ref[...] + sf_ref[...]).astype(bf16)
            g = g_ref[...].astype(f32)
            d_two = norm_back(g * gf_ref[...], normed, rstd)
            dtwo_ref[at] = d_two
            d_ffn = d_two.astype(bf16)
            dffn_ref[at] = d_ffn
            vec_ref[0:1] += jnp.sum(g * normed, 0, keepdims=True)
            vec_ref[1:2] += jnp.sum(g, 0, keepdims=True)
            vec_ref[2:3] += jnp.sum(d_ffn.astype(f32), 0, keepdims=True)


def mid(me, x, ctx, wo, bo, ga, sa, wu, bu, wd, bd, gf, sf, g0, g1):
    rows, width = x.shape
    ff = wu.shape[1]
    cut = ff // 8
    full = pl.BlockSpec((rows, width), lambda j, s: (0, 0))
    col = pl.BlockSpec((rows, 2 * cut), lambda j, s: (0, j))
    vec = shape(3, width, dtype=f32)
    rstd = shape(rows, 1, dtype=f32)
    return call(
        mid_kernel, (2,),
        [full, full, whole(wo), whole(bo), whole(ga), whole(sa)] + quarters(wu, 1, cut)
        + quarters(bu, 1, cut) + quarters(wd, 0, cut) + [whole(bd), whole(gf), whole(sf), whole(g0), whole(g1)],
        [shape(rows, width), shape(rows, width, dtype=f32), rstd] + [shape(rows, ff // 2)] * 4
        + [shape(rows, width), shape(rows, width, dtype=f32), shape(rows, width), vec],
        [full, full, whole(rstd)] + [col] * 4 + [full, full, full, whole(vec)],
        [pltpu.VMEM((rows, width), f32)],
        me, x, ctx, wo, bo, ga, sa, *[wu] * 4, *[bu] * 4, *[wd] * 4, bd, gf, sf, g0, g1,
        micros=18, mib=26,
    )


def back_one_kernel(me, dffn_ref, wd0, wd1, wd2, wd3, dm_ref, dt_ref, pm_ref, pt_ref, vec_ref):
    j = pl.program_id(0)
    d_ffn = dffn_ref[...]
    cut = wd0.shape[0]
    for far, wds, d_ref, p_ref in (
        (0, (wd0, wd1), dm_ref, pm_ref), (1, (wd2, wd3), dt_ref, pt_ref),
    ):
        down = jnp.concatenate([w[...] for w in wds], 0)
        d_pre = (mm(d_ffn, down, NT) * d_ref[...].astype(f32)).astype(bf16)
        p_ref[...] = d_pre
        total = jnp.sum(d_pre.astype(f32), 0, keepdims=True)
        span = pl.ds(pl.multiple_of((me[0] ^ far) * cut, cut), cut)
        for k in range(2):
            vec_ref[pl.ds(2 * j + k, 1), span] = total[:, k * cut : (k + 1) * cut]


def back_one(me, dffn, wd, dm, dt):
    rows, width = dffn.shape
    ff = wd.shape[0]
    cut = ff // 8
    full = pl.BlockSpec((rows, width), lambda j, s: (0, 0))
    col = pl.BlockSpec((rows, 2 * cut), lambda j, s: (0, j))
    vec = shape(4, 2 * cut, dtype=f32)
    return call(
        back_one_kernel, (2,), [full] + quarters(wd, 0, cut) + [col, col],
        [shape(rows, ff // 2), shape(rows, ff // 2), vec], [col, col, whole(vec)],
        [], me, dffn, *[wd] * 4, dm, dt, micros=6,
    )


def back_two_kernel(
    me, pm_ref, pt_ref, wu0, wu1, wu2, wu3, dtwo_ref, n_ref, r_ref, gain_ref, wo_ref,
    done_ref, dattn_ref, dctx_ref, vec_ref, acc,
):
    j = pl.program_id(0)
    part = mm(pm_ref[...], jnp.concatenate([wu0[...], wu1[...]], 1), NT)
    part = part + mm(pt_ref[...], jnp.concatenate([wu2[...], wu3[...]], 1), NT)

    @pl.when(j == 0)
    def _():
        acc[...] = part

    @pl.when(j == 1)
    def _():
        acc[...] += part
        rows = acc.shape[0]
        vec_ref[...] = jnp.zeros_like(vec_ref)
        for i in range(2):
            at = slice(i * (rows // 2), (i + 1) * (rows // 2))
            d_y = acc[at] + dtwo_ref[at]
            normed = n_ref[at]
            d_one = norm_back(d_y * gain_ref[...], normed, r_ref[at])
            done_ref[at] = d_one
            d_attn = d_one.astype(bf16)
            dattn_ref[at] = d_attn
            vec_ref[0:1] += jnp.sum(d_y * normed, 0, keepdims=True)
            vec_ref[1:2] += jnp.sum(d_y, 0, keepdims=True)
            vec_ref[2:3] += jnp.sum(d_attn.astype(f32), 0, keepdims=True)
        dctx_ref[...] = mm(dattn_ref[...], wo_ref[...], NT).astype(bf16)


def back_two(me, pm, pt, wu, dtwo, n, r, gain, wo):
    rows, width = dtwo.shape
    ff = wu.shape[1]
    cut = ff // 8
    full = pl.BlockSpec((rows, width), lambda j, s: (0, 0))
    col = pl.BlockSpec((rows, 2 * cut), lambda j, s: (0, j))
    vec = shape(3, width, dtype=f32)
    return call(
        back_two_kernel, (2,),
        [col, col] + quarters(wu, 1, cut) + [full, full, whole(r), whole(gain), whole(wo)],
        [shape(rows, width, dtype=f32), shape(rows, width), shape(rows, width), vec],
        [full, full, full, whole(vec)],
        [pltpu.VMEM((rows, width), f32)],
        me, pm, pt, *[wu] * 4, dtwo, n, r, gain, wo, micros=8,
    )


def transposed(left, first, second):
    rows = first.shape[0]

    @pl.when(pl.program_id(0) == 0)
    def _():
        left[:, :rows] = jnp.transpose(first[...])
        left[:, rows:] = jnp.transpose(second[...])

    return left[:, :rows], left[:, rows:]


def grad_down_kernel(me, lo_ref, lp_ref, ro_ref, rp_ref, ak, asd, bk, bsd, left, tile):
    lo, lp = transposed(left, lo_ref, lp_ref)
    tile[...] = mm(lo, ro_ref[...]) + mm(lp, rp_ref[...])
    depth = tile.shape[0] // 4
    cols = tile.shape[1] // 2
    size = depth // 2
    for low in range(2):
        k0 = low ^ (me[3] & 1)
        across = slice(low * cols, (low + 1) * cols)
        for xr in range(2):
            for yr in range(2):
                at = pl.multiple_of((2 * (xr ^ me[1]) + (yr ^ me[2])) * depth, size)
                (asd if xr else ak)[yr, k0, 0] = tile[pl.ds(at, size), across].astype(bf16)
                at = pl.multiple_of(at + size, size)
                (bsd if yr else bk)[xr, k0, 0] = tile[pl.ds(at, size), across].astype(bf16)


def grad_down(me, lo, lp, ro, rp):
    rows, width = lo.shape
    cut = ro.shape[1] // 2
    size = width // 8
    full = pl.BlockSpec((rows, width), lambda j, s: (0, 0))
    col = pl.BlockSpec((rows, cut), lambda j, s: (0, j ^ (s[3] >> 1)))
    out = pl.BlockSpec((2, 2, 1, size, cut // 2), lambda j, s: (0, 0, j, 0, 0))
    return call(
        grad_down_kernel, (2,), [full, full, col, col],
        [shape(2, 2, 2, size, cut // 2)] * 4, [out] * 4,
        [pltpu.VMEM((width, 2 * rows), bf16), pltpu.VMEM((width, cut), f32)],
        me, lo, lp, ro, rp, micros=6,
    )


def grad_up_kernel(me, lo_ref, lp_ref, ro_ref, rp_ref, ak, asd, bk, bsd, left, tile):
    lo, lp = transposed(left, lo_ref, lp_ref)
    tile[...] = mm(lo, ro_ref[...]) + mm(lp, rp_ref[...])
    depth = tile.shape[0] // 4
    cols = tile.shape[1] // 2
    size = depth // 2

    def store(a_ref):
        for yr in range(2):
            across = pl.ds(pl.multiple_of((yr ^ me[2]) * cols, 128), cols)
            for zr in range(4):
                at = pl.multiple_of((zr ^ me[3]) * depth, size)
                a_ref[yr, zr & 1, zr >> 1] = tile[pl.ds(at, size), across].astype(bf16)
                at = pl.multiple_of(at + size, size)
                (bsd if yr else bk)[0, zr & 1, zr >> 1] = tile[pl.ds(at, size), across].astype(bf16)

    pl.when(pl.program_id(0) == 0)(lambda: store(ak))
    pl.when(pl.program_id(0) == 1)(lambda: store(asd))


def grad_up(me, lo, lp, ro, rp):
    rows, width = lo.shape
    cut = ro.shape[1] // 2
    size = width // 8
    full = pl.BlockSpec((rows, width), lambda j, s: (0, 0))
    col = pl.BlockSpec((rows, cut), lambda j, s: (0, j ^ s[1]))
    a_out = pl.BlockSpec((2, 2, 2, size, cut // 2), lambda j, s: (0, 0, 0, 0, 0))
    b_out = pl.BlockSpec((1, 2, 2, size, cut // 2), lambda j, s: (j, 0, 0, 0, 0))
    return call(
        grad_up_kernel, (2,), [full, full, col, col],
        [shape(2, 2, 2, size, cut // 2)] * 4, [a_out, a_out, b_out, b_out],
        [pltpu.VMEM((width, 2 * rows), bf16), pltpu.VMEM((width, cut), f32)],
        me, lo, lp, ro, rp, micros=6,
    )


def grad_rest_kernel(
    me, xo_ref, xp_ref, co_ref, cp_ref, qo_ref, qp_ref, ko_ref, kp_ref, vo_ref, vp_ref, ao_ref, ap_ref,
    ak, asd, bk, bsd, left, tile,
):
    rows = xo_ref.shape[0]
    deep = tile.shape[0] // 4
    size = deep // 4
    for t, (own, other) in enumerate(
        ((qo_ref, qp_ref), (ko_ref, kp_ref), (vo_ref, vp_ref), (ao_ref, ap_ref))
    ):
        if t in (0, 3):
            first, second = (co_ref, cp_ref) if t == 3 else (xo_ref, xp_ref)
            left[:, :rows] = jnp.transpose(first[...])
            left[:, rows:] = jnp.transpose(second[...])
        tile[...] = mm(left[:, :rows], own[...]) + mm(left[:, rows:], other[...])
        put = slice((t % 2) * size, (t % 2 + 1) * size)
        for xr in range(2):
            for yr in range(2):
                for zr in range(4):
                    at = (zr ^ me[3]) * deep + (2 * (xr ^ me[1]) + (yr ^ me[2])) * size
                    piece = tile[pl.ds(pl.multiple_of(at, size), size), :].astype(bf16)
                    if t < 2:
                        (asd if xr else ak)[yr, zr & 1, zr >> 1, put] = piece
                    else:
                        (bsd if yr else bk)[xr, zr & 1, zr >> 1, put] = piece


def grad_rest(me, *args):
    rows, width = args[0].shape
    half = width // 2
    dims = (2, 2, 2, width // 8, half)
    return call(
        grad_rest_kernel, (1,), [whole(a) for a in args], [shape(*dims)] * 4,
        [pl.BlockSpec(dims, lambda j, s: (0,) * 5)] * 4,
        [pltpu.VMEM((width, 2 * rows), bf16), pltpu.VMEM((width, half), f32)],
        me, *args, micros=6,
    )


def tok_kernel(me, q0, q1, k0, k1, v0, v1, wq_ref, wk_ref, wv_ref, done_ref, out_ref):
    total = done_ref[...]
    for first, second, w_ref in ((q0, q1, wq_ref), (k0, k1, wk_ref), (v0, v1, wv_ref)):
        total = total + mm(jnp.concatenate([first[...], second[...]], 1), w_ref[...], NT)
    out_ref[...] = total.astype(bf16)


def tok(me, parts, w, done):
    rows, width = done.shape
    thirds = [pl.BlockSpec((width, width), lambda j, s, t=t: (0, t)) for t in range(3)]
    return call(
        tok_kernel, (1,), [whole(a) for a in parts] + thirds + [whole(done)],
        shape(rows, width), pl.BlockSpec((rows, width), lambda j, s: (0, 0)), [],
        me, *parts, w, w, w, done, micros=5,
    )


def gathered(me, refs, held):
    for core in range(2):
        for xr in range(2):
            for yr in range(2):
                held[core ^ me[0], xr ^ me[1], yr ^ me[2]] = refs[4 * core + 2 * xr + yr][...]
    return [(core, p, held[core, p >> 1, p & 1]) for core in range(2) for p in range(4)]


def place_down_kernel(me, *refs):
    *refs, out_ref, held = refs
    for core, p, piece in gathered(me, refs, held):
        rows, cols = piece.shape
        at = slice(core * cols, (core + 1) * cols)
        out_ref[at, p * rows : (p + 1) * rows] = jnp.transpose(piece.astype(f32))


def place_up_kernel(me, *refs):
    *refs, out_ref, held = refs
    for core, p, piece in gathered(me, refs, held):
        cols = piece.shape[1]
        start = (2 * p + core) * cols
        out_ref[:, start : start + cols] = piece.astype(f32)


def place_rest_kernel(me, *refs):
    *refs, qkv_ref, out_ref, held = refs
    for core, p, piece in gathered(me, refs, held):
        cols = piece.shape[1]
        size = piece.shape[0] // 4
        at = slice(p * size, (p + 1) * size)
        for t in range(4):
            start = core * cols + (2 * t * cols if t < 3 else 0)
            part = piece[t * size : (t + 1) * size].astype(f32)
            (qkv_ref if t < 3 else out_ref)[at, start : start + cols] = part


def place_vec_kernel(me, a_ref, b_ref, c_ref, d_ref, *outs):
    total = (a_ref[...] + b_ref[...]) + (c_ref[...] + d_ref[...])
    cut = total.shape[1] // 4
    for z in range(4):
        @pl.when(me[3] == z)
        def _():
            for i in range(8):
                outs[i][...] = total[i : i + 1, z * cut : (z + 1) * cut]
            outs[8][...] = total[8 + z : 9 + z]


def place_vec(me, parts):
    width = parts[0].shape[1]
    outs = [shape(1, width // 4, dtype=f32)] * 8 + [shape(1, width, dtype=f32)]
    return call(
        place_vec_kernel, (1,), [whole(a) for a in parts], outs,
        [whole(o) for o in outs], [], me, *parts, micros=1, mib=16,
    )


def place(me, kernel, outs, parts):
    outs = [shape(*dims, dtype=f32) for dims in outs]
    rows, cols = parts[0].shape
    return call(
        kernel, (1,), [whole(a) for a in parts], outs, [whole(o) for o in outs],
        [pltpu.VMEM((2, 2, 2, rows, cols), bf16)], me, *parts, micros=3, mib=16,
    )


def local(
    dp, seq, tokens, lengths, head_swap, w_qkv, bias_q, bias_v, w_out, bias_out, gain_attn,
    shift_attn, w_up, bias_up, w_down, bias_down, gain_ffn, shift_ffn, cotangent,
):
    seqs_here, part_len, width = tokens.shape
    heads = head_swap.shape[0]
    head_dim = width // heads
    rows = seqs_here * part_len
    assert seqs_here == 2 and seq == 4 and dp % 8 == 0
    spot = lax.axis_index("dp")
    z = lax.axis_index("seq")
    core = spot & 1
    odd = z & 1
    me = jnp.stack([core, (spot >> 1) & 1, (spot >> 2) & 1, z]).astype(jnp.int32)

    def over_dp(arr, bit):
        return lax.ppermute(arr, "dp", [(i, i ^ bit) for i in range(dp)])

    def over_seq(arr, bit):
        return lax.ppermute(arr, "seq", [(i, i ^ bit) for i in range(seq)])

    def other(arr):
        return over_dp(arr, 1)

    def tie(value, *others):
        return lax.optimization_barrier((value, others))[0]

    def there(i, r):
        d, k = divmod(i, seq)
        return ((d & ~1) | (k >> 1)) * seq + 2 * (d & 1) + (r ^ (k & 1))

    ways = [[(i, there(i, r)) for i in range(dp * seq)] for r in range(2)]

    def send_block(parts):
        out = []
        for r, part in enumerate(parts):
            out.append(lax.ppermute(part, ("dp", "seq"), ways[r]))
        return out

    def gather_block(arr):
        return send_block([lax.dynamic_index_in_dim(arr, r ^ odd, 0, False) for r in range(2)])

    def return_block(arr):
        back = []
        for r in range(2):
            part = arr[r * part_len : (r + 1) * part_len]
            back.append(lax.ppermute(part, ("dp", "seq"), [(b, a) for a, b in ways[r]]))
        return back

    def in_order(back):
        return jnp.where(odd_z, jnp.stack(back[::-1]), jnp.stack(back))

    near = gather_block(tokens)
    length = lax.ppermute(lax.dynamic_slice_in_dim(lengths, odd, 1, 0), ("dp", "seq"), ways[0])[0]

    def limit(block, half):
        return length - (block * rows + (half ^ odd) * part_len)

    info = jnp.concatenate(
        [
            jnp.stack([limit(core, 0), limit(core, 1), limit(1 - core, 0), limit(1 - core, 1)]),
            head_swap,
        ]
    ).astype(jnp.int32)
    far = jnp.repeat(head_swap, head_dim)[None, :] == 1
    given = [lax.dynamic_index_in_dim(cotangent, r ^ odd, 0, False) for r in range(2)]
    near, info, far, me, second, odd_z, given = tie(
        (near, info, far, me, core == 1, odd == 1, given)
    )
    x = jnp.concatenate(near, 0)
    x_far = other(x)
    grad = send_block(tie(given, x))

    q = (mm(x, w_qkv[:, :width]) + bias_q).astype(bf16) * bf16(head_dim**-0.5)
    w_k, w_v = w_qkv[:, width : 2 * width], w_qkv[:, 2 * width :]
    k = jnp.where(far, mm(x_far, w_k), mm(x, w_k)).astype(bf16)
    v = (jnp.where(far, mm(x_far, w_v), mm(x, w_v)) + bias_v).astype(bf16)
    ctx, probs = attn_fwd(info, q, k, v)
    ctx_far = other(ctx)
    y, normed, rstd, act_m, act_t, slope_m, slope_t, out, d_two, d_ffn, vec_two = mid(
        me, x, ctx, w_out, bias_out[None], gain_attn[None], shift_attn[None], w_up, bias_up[None],
        w_down, bias_down[None], gain_ffn[None], shift_ffn[None], *grad,
    )

    def add(a, b):
        return (a.astype(f32) + b.astype(f32)).astype(bf16)

    def halve_first(stored):
        a_keep, a_send, b_keep, b_send = stored
        return (add(a_keep, over_dp(a_send, 2)), add(b_keep, over_dp(b_send, 4)))

    def halve_second(pair):
        a, b = pair
        return (add(a[0], over_dp(a[1], 4)), add(b[0], over_dp(b[1], 2)))

    def halve_seq_first(c):
        return add(c[0], over_seq(c[1], 1))

    def halve_seq_second(c):
        c = add(c[0], over_seq(c[1], 2))
        bit = 8
        while bit < dp:
            c = add(c, over_dp(c, bit))
            bit *= 2
        return c

    def collect(c, *others):
        c = c.reshape(-1, c.shape[-1])
        own = [c] + [over_dp(c, bit) for bit in (4, 2, 6)]
        if others:
            own = tie(own, *others)
        return own + [other(o) for o in own]

    half = width // 2
    d_ffn_far = other(d_ffn)
    act_far = other(act_t)
    y_far = other(y)
    pre_m, pre_t, vec_up = back_one(me, d_ffn, w_down, slope_m, slope_t)
    pre_far = other(pre_t)
    output = return_block(tie(out, pre_m))
    down = grad_down(me, d_ffn, d_ffn_far, act_m, act_far)
    pre_m, down = tie((pre_m, down))
    down = halve_first(down)
    d_one, d_attn, d_ctx, vec_one = back_two(
        me, pre_m, pre_t, w_up, d_two, normed, rstd, gain_attn[None], w_out
    )

    def mine(pair):
        return jnp.where(second, pair[1], pair[0])

    heads_far = [far[:, :half], far[:, half:]]
    pairs = heads // 4
    qs, ks, vs, k_gots, v_gots, vecs = [], [], [], [], [], []
    for i in range(2):
        d_q, d_k, d_v, vec = attn_bwd(info, i * pairs, pairs, q, k, v, d_ctx, probs)
        qs.append(d_q)
        ks.append(d_k)
        vs.append(d_v)
        vecs.append(vec)
        k_gots.append(other(d_k))
        v_gots.append(other(d_v))
        if i == 0:
            attn_far = other(jnp.where(second, d_attn[:, :half], d_attn[:, half:]))
            d_ctx, down, d_q = tie((d_ctx, down, d_q))
            down = halve_second(down)
    q_far = other(jnp.where(second, qs[0], qs[1]))
    down, qs = tie((down, qs))
    down = halve_seq_first(jnp.stack(down, 2))
    up = grad_up(me, y, y_far, pre_m, pre_far)
    down, up = tie((down, up))
    down = halve_seq_second(down)
    up = halve_first(up)
    k_own = [jnp.where(f, g, u) for f, g, u in zip(heads_far, k_gots, ks)]
    k_oth = [jnp.where(f, u, g) for f, g, u in zip(heads_far, k_gots, ks)]
    v_own = [jnp.where(f, g, u) for f, g, u in zip(heads_far, v_gots, vs)]
    v_oth = [jnp.where(f, u, g) for f, g, u in zip(heads_far, v_gots, vs)]

    rest = grad_rest(
        me, x, x_far, ctx, ctx_far, mine(qs), q_far, mine(k_own), mine(k_oth), mine(v_own),
        mine(v_oth), mine((d_attn[:, :half], d_attn[:, half:])), attn_far,
    )
    rest, qs, vecs = tie((rest, qs, vecs))
    rest = halve_first(rest)
    d_tok = tok(me, qs + k_own + v_own, w_qkv, d_one)
    d_tok = return_block(d_tok)
    up = halve_second(up)
    vec = jnp.concatenate(
        [jnp.concatenate(vecs, 1), vec_one, vec_two, vec_up], 0
    )
    vec = vec + other(vec)
    bit = 8
    while bit < dp:
        vec = vec + over_dp(vec, bit)
        bit *= 2
    v_y, v_x, v_d = tie([over_dp(vec, bit) for bit in (4, 2, 6)], rest)
    (s_down,) = place(me, place_down_kernel, [(width, width)], collect(down))
    up = halve_seq_first(jnp.stack(up, 2))
    rest = halve_second(rest)
    vec = (vec + v_y) + (v_x + v_d)
    vec_z = [vec] + [over_seq(vec, bit) for bit in (1, 2, 3)]
    rest = halve_seq_first(jnp.stack(rest, 2))
    up = halve_seq_second(up)
    (s_up,) = place(me, place_up_kernel, [(width // seq, w_up.shape[1])], collect(up))
    rest = tie(halve_seq_second(rest), s_down)
    rest = collect(rest, s_up)
    s_qkv, s_out = place(
        me, place_rest_kernel, [(width // seq, 3 * width), (width // seq, width)], rest
    )
    output = in_order(output)
    d_tokens = in_order(d_tok).astype(f32)

    s_bq, s_bv, s_ga, s_sa, s_bo, s_gf, s_sf, s_bd, s_b_up = (
        v.reshape(-1) for v in place_vec(me, vec_z)
    )
    return (
        output, d_tokens, s_qkv, s_bq, s_bv, s_out, s_bo, s_ga, s_sa, s_up, s_b_up, s_down, s_bd,
        s_gf, s_sf,
    )


def solution(mesh):
    dp, seq = mesh.shape["dp"], mesh.shape["seq"]
    rows = P("dp", "seq", None)
    placed = (rows, P("dp")) + (P(),) * 14 + (rows,)
    cut, line = P("seq", None), P("seq")

    def body(*args):
        return local(dp, seq, *args)

    return jax.shard_map(
        body,
        mesh=mesh,
        in_specs=placed,
        out_specs=(
            rows, rows, cut, line, line, cut, line, line, line, cut, line, cut, line, line, line,
        ),
        check_vma=False,
    )
```

```python
import functools

import jax
import jax.numpy as jnp
from jax import lax
from jax.experimental import pallas as pl
from jax.experimental.pallas import tpu as pltpu
from jax.sharding import PartitionSpec as P


f32 = jnp.float32
bf16 = jnp.bfloat16
NN = (((1,), (0,)), ((), ()))
NT = (((1,), (1,)), ((), ()))
TN = (((0,), (0,)), ((), ()))

CHUNK = 256


def mm(a, b, dims=NN):
    return lax.dot_general(a, b, dims, preferred_element_type=f32)


def shape(*dims, dtype=bf16):
    return jax.ShapeDtypeStruct(dims, dtype)


def whole(arr):
    zeros = (0,) * arr.ndim
    return pl.BlockSpec(arr.shape, lambda *_: zeros)


def call(kernel, grid, specs, outs, out_specs, scratch, scalars, *args, micros=8, mib=16):
    return pl.pallas_call(
        kernel,
        grid_spec=pltpu.PrefetchScalarGridSpec(
            num_scalar_prefetch=1,
            grid=grid,
            in_specs=specs,
            out_specs=out_specs,
            scratch_shapes=scratch,
        ),
        out_shape=outs,
        cost_estimate=pl.CostEstimate(
            flops=micros * 1_000_000_000, bytes_accessed=8_000_000, transcendentals=0
        ),
        compiler_params=pltpu.CompilerParams(vmem_limit_bytes=mib << 20),
    )(scalars, *args)


def limits(info, pair, h, place, half):
    swap = info[4 + 2 * pair + h]
    first = jnp.where(swap == 1, info[2], info[0])
    second = jnp.where(swap == 1, info[3], info[1])
    return place < jnp.where(place < half, first, second + half)


def qkv_kernel(info, x_ref, xf_ref, w_ref, far_ref, bias_ref, q_ref, k_ref, v_ref, near):
    t = pl.program_id(0)
    near[...] = mm(x_ref[...], w_ref[...])

    @pl.when(t == 0)
    def _():
        scale = bf16((q_ref.shape[1] // (info.shape[0] - 4)) ** -0.5)
        q_ref[...] = (near[...] + bias_ref[0]).astype(bf16) * scale

    @pl.when(t > 0)
    def _():
        picked = jnp.where(far_ref[...] == 1, mm(xf_ref[...], w_ref[...]), near[...])
        picked = (picked + bias_ref[0]).astype(bf16)
        for i, out_ref in ((1, k_ref), (2, v_ref)):
            @pl.when(t == i)
            def _():
                out_ref[...] = picked


def qkv(info, x, x_far, w, far, bias):
    rows, width = x.shape
    full = pl.BlockSpec((rows, width), lambda j, s: (0, 0))
    return call(
        qkv_kernel, (3,),
        [full, full, pl.BlockSpec((width, width), lambda j, s: (0, j)), whole(far),
         pl.BlockSpec((1, 1, width), lambda j, s: (j, 0, 0))],
        [shape(rows, width)] * 3, [full] * 3, [pltpu.VMEM((rows, width), f32)],
        info, x, x_far, w, far, bias, micros=5,
    )


def attn_fwd_kernel(info, q_ref, k_ref, v_ref, ctx_ref, p_ref):
    rows = q_ref.shape[0]
    lanes = 128
    hd = lanes // 2
    lane = lax.broadcasted_iota(jnp.int32, (rows, lanes), 1)
    place = lax.broadcasted_iota(jnp.int32, (rows, rows), 0)
    count = q_ref.shape[1] // lanes
    for i in range(count):
        cols = slice(i * lanes, (i + 1) * lanes)
        q = q_ref[:, cols]
        k = k_ref[:, cols]
        v = v_ref[:, cols]
        parts = []
        for h in range(2):
            mine = (lane < hd) if h == 0 else (lane >= hd)
            s = mm(jnp.where(mine, k, jnp.zeros_like(k)), q, NT)
            ok = limits(info, pl.program_id(0) * count + i, h, place, rows // 2)
            s = jnp.where(ok, s, f32(-10000.0))
            e = jnp.exp(s - jnp.max(s, 0, keepdims=True))
            p = (e * (1.0 / jnp.sum(e, 0, keepdims=True))).astype(bf16)
            p_ref[2 * i + h] = p
            parts.append(mm(p, v, TN))
        ctx_ref[:, cols] = jnp.where(lane < hd, parts[0], parts[1]).astype(bf16)


def attn_fwd(info, q, k, v):
    rows, width = q.shape
    pairs = width // 128
    blk = pl.BlockSpec((rows, 256), lambda j, s: (0, j))
    sq = pl.BlockSpec((4, rows, rows), lambda j, s: (j, 0, 0))
    return call(
        attn_fwd_kernel, (pairs // 2,), [blk] * 3,
        [shape(rows, width), pltpu.HBM((2 * pairs, rows, rows), bf16)], [blk, sq], [], info, q, k, v,
    )


def attn_bwd_kernel(
    start, info, q_ref, k_ref, v_ref, g_ref, c_ref, p_ref, dq_ref, dk_ref, dv_ref, vec_ref
):
    pair = pl.program_id(0) + start
    rows, lanes = q_ref.shape
    hd = lanes // 2
    lane = lax.broadcasted_iota(jnp.int32, (rows, lanes), 1)
    place = lax.broadcasted_iota(jnp.int32, (rows, lanes), 0)
    q = q_ref[...]
    k = k_ref[...]
    v = v_ref[...]
    g = g_ref[...]
    zero = jnp.zeros_like(k)
    oks = [limits(info, pair, h, place, rows // 2) for h in range(2)]
    ok = jnp.where(lane < hd, jnp.where(oks[0], 1, 0), jnp.where(oks[1], 1, 0)) == 1
    kt = jnp.transpose(jnp.where(ok, k, zero))
    dvs, dks, dqs = [], [], []
    prod = jnp.transpose(g.astype(f32) * c_ref[...].astype(f32))
    for h in range(2):
        mine = (lane < hd) if h == 0 else (lane >= hd)
        dp = mm(jnp.where(mine, v, zero), g, NT)
        pb = p_ref[h]
        p = pb.astype(f32)
        inner = jnp.sum(prod[h * hd : (h + 1) * hd], 0, keepdims=True)
        ds = (p * (dp - inner)).astype(bf16)
        dvs.append(mm(pb, g))
        dks.append(mm(ds, q))
        dqs.append(mm(kt[h * hd : (h + 1) * hd], ds))
    dv = jnp.where(lane < hd, dvs[0], dvs[1]).astype(bf16)
    dq = (jnp.transpose(jnp.concatenate(dqs, 0)) * f32(hd**-0.5)).astype(bf16)
    dv_ref[...] = dv
    dk_ref[...] = jnp.where(ok, jnp.where(lane < hd, dks[0], dks[1]), f32(0.0)).astype(bf16)
    dq_ref[...] = dq
    vec_ref[0:1] = jnp.sum(dq.astype(f32), 0, keepdims=True)
    vec_ref[1:2] = jnp.sum(dv.astype(f32), 0, keepdims=True)


def attn_bwd(info, first, pairs, q, k, v, g, c, p):
    rows = q.shape[0]
    blk = pl.BlockSpec((rows, 128), lambda j, s: (0, j + first))
    sq = pl.BlockSpec((2, rows, rows), lambda j, s: (j + first, 0, 0))
    out = pl.BlockSpec((rows, 128), lambda j, s: (0, j))
    return call(
        functools.partial(attn_bwd_kernel, first), (pairs,), [blk] * 5 + [sq],
        [shape(rows, 128 * pairs)] * 3 + [shape(2, 128 * pairs, dtype=f32)],
        [out] * 3 + [pl.BlockSpec((2, 128), lambda j, s: (0, j))],
        [], info, q, k, v, g, c, p, micros=6, mib=16,
    )


def normalize(hidden):
    center = hidden - jnp.mean(hidden, -1, keepdims=True)
    rstd = lax.rsqrt(jnp.mean(center * center, -1, keepdims=True) + 1e-05)
    return center * rstd, rstd


def norm_back(scaled, normed, rstd):
    return rstd * (
        scaled
        - jnp.mean(scaled, -1, keepdims=True)
        - normed * jnp.mean(scaled * normed, -1, keepdims=True)
    )


def by_rows(rows, size, body):
    def step(i, carry):
        body(pl.ds(pl.multiple_of(i * size, size), size))
        return carry

    lax.fori_loop(0, rows // size, step, 0)


def gelu_both(x):
    t = 1.0 / (1.0 + f32(0.3275911 * 0.7071067811865476) * jnp.abs(x))
    poly = f32(-1.453152027 / 2) + t * f32(1.061405429 / 2)
    poly = f32(1.421413741 / 2) + t * poly
    poly = f32(-0.284496736 / 2) + t * poly
    poly = t * (f32(0.254829592 / 2) + t * poly)
    bell = jnp.exp(x * x * f32(-0.5))
    tail = poly * bell
    dist = jnp.where(x >= 0, 1.0 - tail, tail)
    return x * dist, dist + x * bell * f32(0.3989422804014327)


def quarters(array, axis, cut):
    specs = []
    for far in range(2):
        for k in range(2):
            def index(j, s, far=far, k=k):
                at = 2 * (2 * j + k) + (s[0] ^ far)
                return (at, 0) if axis == 0 else (0, at)

            dims = list(array.shape)
            dims[axis] = cut
            specs.append(pl.BlockSpec(tuple(dims), index))
    return specs


def mid_kernel(
    me, x_ref, ctx_ref, wo_ref, bo_ref, ga_ref, sa_ref, wu0, wu1, wu2, wu3, bu0, bu1, bu2, bu3,
    wd0, wd1, wd2, wd3, bd_ref, gf_ref, sf_ref, g0_ref, g1_ref,
    y_ref, n_ref, r_ref, am_ref, at_ref, dm_ref, dt_ref, out_ref, dtwo_ref, dffn_ref, vec_ref,
    acc, grad,
):
    j = pl.program_id(0)
    rows = x_ref.shape[0]
    part_len = rows // 2

    @pl.when(j == 0)
    def _():
        acc[...] = mm(ctx_ref[...], wo_ref[...])

        def first(at):
            normed, rstd = normalize(x_ref[at].astype(f32) + (acc[at] + bo_ref[...]))
            n_ref[at] = normed
            r_ref[at] = rstd
            y_ref[at] = (normed * ga_ref[...] + sa_ref[...]).astype(bf16)

        by_rows(rows, CHUNK // 2, first)

    y = y_ref[...]
    part = None
    for wus, bus, wds, a_ref, d_ref in (
        ((wu0, wu1), (bu0, bu1), (wd0, wd1), am_ref, dm_ref),
        ((wu2, wu3), (bu2, bu3), (wd2, wd3), at_ref, dt_ref),
    ):
        up = jnp.concatenate([w[...] for w in wus], 1)
        pre = mm(y, up) + jnp.concatenate([b[...] for b in bus], 1)
        act, slope = gelu_both(pre)
        act = act.astype(bf16)
        a_ref[...] = act
        d_ref[...] = slope.astype(bf16)
        more = mm(act, jnp.concatenate([w[...] for w in wds], 0))
        part = more if part is None else part + more

    @pl.when(j == 0)
    def _():
        acc[...] = part

    @pl.when(j == 1)
    def _():
        acc[...] += part
        vec_ref[...] = jnp.zeros_like(vec_ref)
        grad[:part_len] = g0_ref[...]
        grad[part_len:] = g1_ref[...]

        def second(at):
            normed, rstd = normalize(y_ref[at].astype(f32) + (acc[at] + bd_ref[...]))
            out_ref[at] = (normed * gf_ref[...] + sf_ref[...]).astype(bf16)
            g = grad[at].astype(f32)
            d_two = norm_back(g * gf_ref[...], normed, rstd)
            dtwo_ref[at] = d_two
            d_ffn = d_two.astype(bf16)
            dffn_ref[at] = d_ffn
            vec_ref[0:1] += jnp.sum(g * normed, 0, keepdims=True)
            vec_ref[1:2] += jnp.sum(g, 0, keepdims=True)
            vec_ref[2:3] += jnp.sum(d_ffn.astype(f32), 0, keepdims=True)

        by_rows(rows, CHUNK, second)


def mid(me, x, ctx, wo, bo, ga, sa, wu, bu, wd, bd, gf, sf, g0, g1):
    rows, width = x.shape
    ff = wu.shape[1]
    cut = ff // 8
    full = pl.BlockSpec((rows, width), lambda j, s: (0, 0))
    col = pl.BlockSpec((rows, 2 * cut), lambda j, s: (0, j))
    vec = shape(3, width, dtype=f32)
    rstd = shape(rows, 1, dtype=f32)
    return call(
        mid_kernel, (2,),
        [full, full, whole(wo), whole(bo), whole(ga), whole(sa)] + quarters(wu, 1, cut)
        + quarters(bu, 1, cut) + quarters(wd, 0, cut) + [whole(bd), whole(gf), whole(sf), whole(g0), whole(g1)],
        [shape(rows, width), shape(rows, width, dtype=f32), rstd] + [shape(rows, ff // 2)] * 4
        + [shape(rows, width), shape(rows, width, dtype=f32), shape(rows, width), vec],
        [full, full, whole(rstd)] + [col] * 4 + [full, full, full, whole(vec)],
        [pltpu.VMEM((rows, width), f32), pltpu.VMEM((rows, width), bf16)],
        me, x, ctx, wo, bo, ga, sa, *[wu] * 4, *[bu] * 4, *[wd] * 4, bd, gf, sf, g0, g1,
        micros=18, mib=26,
    )


def back_one_kernel(me, dffn_ref, wd0, wd1, wd2, wd3, dm_ref, dt_ref, pm_ref, pt_ref, vec_ref):
    j = pl.program_id(0)
    d_ffn = dffn_ref[...]
    cut = wd0.shape[0]
    for far, wds, d_ref, p_ref in (
        (0, (wd0, wd1), dm_ref, pm_ref), (1, (wd2, wd3), dt_ref, pt_ref),
    ):
        down = jnp.concatenate([w[...] for w in wds], 0)
        d_pre = (mm(d_ffn, down, NT) * d_ref[...].astype(f32)).astype(bf16)
        p_ref[...] = d_pre
        total = jnp.sum(d_pre.astype(f32), 0, keepdims=True)
        span = pl.ds(pl.multiple_of((me[0] ^ far) * cut, cut), cut)
        for k in range(2):
            vec_ref[pl.ds(2 * j + k, 1), span] = total[:, k * cut : (k + 1) * cut]


def back_one(me, dffn, wd, dm, dt):
    rows, width = dffn.shape
    ff = wd.shape[0]
    cut = ff // 8
    full = pl.BlockSpec((rows, width), lambda j, s: (0, 0))
    col = pl.BlockSpec((rows, 2 * cut), lambda j, s: (0, j))
    vec = shape(4, 2 * cut, dtype=f32)
    return call(
        back_one_kernel, (2,), [full] + quarters(wd, 0, cut) + [col, col],
        [shape(rows, ff // 2), shape(rows, ff // 2), vec], [col, col, whole(vec)],
        [], me, dffn, *[wd] * 4, dm, dt, micros=6,
    )


def back_two_kernel(
    me, pm_ref, pt_ref, wu0, wu1, wu2, wu3, dtwo_ref, n_ref, r_ref, gain_ref, wo_ref,
    done_ref, dattn_ref, dctx_ref, vec_ref, acc,
):
    j = pl.program_id(0)
    part = mm(pm_ref[...], jnp.concatenate([wu0[...], wu1[...]], 1), NT)
    part = part + mm(pt_ref[...], jnp.concatenate([wu2[...], wu3[...]], 1), NT)

    @pl.when(j == 0)
    def _():
        acc[...] = part

    @pl.when(j == 1)
    def _():
        acc[...] += part
        rows = acc.shape[0]
        vec_ref[...] = jnp.zeros_like(vec_ref)

        def last(at):
            d_y = acc[at] + dtwo_ref[at]
            normed = n_ref[at]
            d_one = norm_back(d_y * gain_ref[...], normed, r_ref[at])
            done_ref[at] = d_one
            d_attn = d_one.astype(bf16)
            dattn_ref[at] = d_attn
            vec_ref[0:1] += jnp.sum(d_y * normed, 0, keepdims=True)
            vec_ref[1:2] += jnp.sum(d_y, 0, keepdims=True)
            vec_ref[2:3] += jnp.sum(d_attn.astype(f32), 0, keepdims=True)

        by_rows(rows, CHUNK, last)
        dctx_ref[...] = mm(dattn_ref[...], wo_ref[...], NT).astype(bf16)


def back_two(me, pm, pt, wu, dtwo, n, r, gain, wo):
    rows, width = dtwo.shape
    ff = wu.shape[1]
    cut = ff // 8
    full = pl.BlockSpec((rows, width), lambda j, s: (0, 0))
    col = pl.BlockSpec((rows, 2 * cut), lambda j, s: (0, j))
    vec = shape(3, width, dtype=f32)
    return call(
        back_two_kernel, (2,),
        [col, col] + quarters(wu, 1, cut) + [full, full, whole(r), whole(gain), whole(wo)],
        [shape(rows, width, dtype=f32), shape(rows, width), shape(rows, width), vec],
        [full, full, full, whole(vec)],
        [pltpu.VMEM((rows, width), f32)],
        me, pm, pt, *[wu] * 4, dtwo, n, r, gain, wo, micros=8,
    )


def transposed(left, first, second):
    rows = first.shape[0]

    @pl.when(pl.program_id(0) == 0)
    def _():
        left[:, :rows] = jnp.transpose(first[...])
        left[:, rows:] = jnp.transpose(second[...])

    return left[:, :rows], left[:, rows:]


def grad_down_kernel(me, lo_ref, lp_ref, ro_ref, rp_ref, ak, asd, bk, bsd, left, tile):
    lo, lp = transposed(left, lo_ref, lp_ref)
    tile[...] = mm(lo, ro_ref[...]) + mm(lp, rp_ref[...])
    depth = tile.shape[0] // 4
    cols = tile.shape[1] // 2
    size = depth // 2
    for low in range(2):
        k0 = low ^ (me[3] & 1)
        across = slice(low * cols, (low + 1) * cols)
        for xr in range(2):
            for yr in range(2):
                at = pl.multiple_of((2 * (xr ^ me[1]) + (yr ^ me[2])) * depth, size)
                (asd if xr else ak)[yr, k0, 0] = tile[pl.ds(at, size), across].astype(bf16)
                at = pl.multiple_of(at + size, size)
                (bsd if yr else bk)[xr, k0, 0] = tile[pl.ds(at, size), across].astype(bf16)


def grad_down(me, lo, lp, ro, rp):
    rows, width = lo.shape
    cut = ro.shape[1] // 2
    size = width // 8
    full = pl.BlockSpec((rows, width), lambda j, s: (0, 0))
    col = pl.BlockSpec((rows, cut), lambda j, s: (0, j ^ (s[3] >> 1)))
    out = pl.BlockSpec((2, 2, 1, size, cut // 2), lambda j, s: (0, 0, j, 0, 0))
    return call(
        grad_down_kernel, (2,), [full, full, col, col],
        [shape(2, 2, 2, size, cut // 2)] * 4, [out] * 4,
        [pltpu.VMEM((width, 2 * rows), bf16), pltpu.VMEM((width, cut), f32)],
        me, lo, lp, ro, rp, micros=6,
    )


def grad_up_kernel(me, lo_ref, lp_ref, ro_ref, rp_ref, ak, asd, bk, bsd, left, tile):
    lo, lp = transposed(left, lo_ref, lp_ref)
    tile[...] = mm(lo, ro_ref[...]) + mm(lp, rp_ref[...])
    depth = tile.shape[0] // 4
    cols = tile.shape[1] // 2
    size = depth // 2

    def store(a_ref):
        for yr in range(2):
            across = pl.ds(pl.multiple_of((yr ^ me[2]) * cols, 128), cols)
            for zr in range(4):
                at = pl.multiple_of((zr ^ me[3]) * depth, size)
                a_ref[yr, zr & 1, zr >> 1] = tile[pl.ds(at, size), across].astype(bf16)
                at = pl.multiple_of(at + size, size)
                (bsd if yr else bk)[0, zr & 1, zr >> 1] = tile[pl.ds(at, size), across].astype(bf16)

    pl.when(pl.program_id(0) == 0)(lambda: store(ak))
    pl.when(pl.program_id(0) == 1)(lambda: store(asd))


def grad_up(me, lo, lp, ro, rp):
    rows, width = lo.shape
    cut = ro.shape[1] // 2
    size = width // 8
    full = pl.BlockSpec((rows, width), lambda j, s: (0, 0))
    col = pl.BlockSpec((rows, cut), lambda j, s: (0, j ^ s[1]))
    a_out = pl.BlockSpec((2, 2, 2, size, cut // 2), lambda j, s: (0, 0, 0, 0, 0))
    b_out = pl.BlockSpec((1, 2, 2, size, cut // 2), lambda j, s: (j, 0, 0, 0, 0))
    return call(
        grad_up_kernel, (2,), [full, full, col, col],
        [shape(2, 2, 2, size, cut // 2)] * 4, [a_out, a_out, b_out, b_out],
        [pltpu.VMEM((width, 2 * rows), bf16), pltpu.VMEM((width, cut), f32)],
        me, lo, lp, ro, rp, micros=6,
    )


def grad_rest_kernel(
    me, xo_ref, xp_ref, co_ref, cp_ref, qo_ref, qp_ref, ko_ref, kp_ref, vo_ref, vp_ref, ao_ref, ap_ref,
    ak, asd, bk, bsd, left, tile,
):
    rows = xo_ref.shape[0]
    deep = tile.shape[0] // 4
    size = deep // 4
    for t, (own, other) in enumerate(
        ((qo_ref, qp_ref), (ko_ref, kp_ref), (vo_ref, vp_ref), (ao_ref, ap_ref))
    ):
        if t in (0, 3):
            first, second = (co_ref, cp_ref) if t == 3 else (xo_ref, xp_ref)
            left[:, :rows] = jnp.transpose(first[...])
            left[:, rows:] = jnp.transpose(second[...])
        tile[...] = mm(left[:, :rows], own[...]) + mm(left[:, rows:], other[...])
        put = slice((t % 2) * size, (t % 2 + 1) * size)
        for xr in range(2):
            for yr in range(2):
                for zr in range(4):
                    at = (zr ^ me[3]) * deep + (2 * (xr ^ me[1]) + (yr ^ me[2])) * size
                    piece = tile[pl.ds(pl.multiple_of(at, size), size), :].astype(bf16)
                    if t < 2:
                        (asd if xr else ak)[yr, zr & 1, zr >> 1, put] = piece
                    else:
                        (bsd if yr else bk)[xr, zr & 1, zr >> 1, put] = piece


def grad_rest(me, *args):
    rows, width = args[0].shape
    half = width // 2
    dims = (2, 2, 2, width // 8, half)
    return call(
        grad_rest_kernel, (1,), [whole(a) for a in args], [shape(*dims)] * 4,
        [pl.BlockSpec(dims, lambda j, s: (0,) * 5)] * 4,
        [pltpu.VMEM((width, 2 * rows), bf16), pltpu.VMEM((width, half), f32)],
        me, *args, micros=6,
    )


def tok_kernel(me, q0, q1, k0, k1, v0, v1, wq_ref, wk_ref, wv_ref, done_ref, out_ref):
    total = done_ref[...]
    for first, second, w_ref in ((q0, q1, wq_ref), (k0, k1, wk_ref), (v0, v1, wv_ref)):
        total = total + mm(jnp.concatenate([first[...], second[...]], 1), w_ref[...], NT)
    out_ref[...] = total.astype(bf16)


def tok(me, parts, w, done):
    rows, width = done.shape
    thirds = [pl.BlockSpec((width, width), lambda j, s, t=t: (0, t)) for t in range(3)]
    return call(
        tok_kernel, (1,), [whole(a) for a in parts] + thirds + [whole(done)],
        shape(rows, width), pl.BlockSpec((rows, width), lambda j, s: (0, 0)), [],
        me, *parts, w, w, w, done, micros=5,
    )


def gathered(me, refs, held):
    for core in range(2):
        for xr in range(2):
            for yr in range(2):
                held[core ^ me[0], xr ^ me[1], yr ^ me[2]] = refs[4 * core + 2 * xr + yr][...]
    return [(core, p, held[core, p >> 1, p & 1]) for core in range(2) for p in range(4)]


def place_down_kernel(me, *refs):
    *refs, out_ref, held = refs
    for core, p, piece in gathered(me, refs, held):
        rows, cols = piece.shape
        at = slice(core * cols, (core + 1) * cols)
        out_ref[at, p * rows : (p + 1) * rows] = jnp.transpose(piece.astype(f32))


def place_up_kernel(me, *refs):
    *refs, out_ref, held = refs
    for core, p, piece in gathered(me, refs, held):
        cols = piece.shape[1]
        start = (2 * p + core) * cols
        out_ref[:, start : start + cols] = piece.astype(f32)


def place_rest_kernel(me, *refs):
    *refs, qkv_ref, out_ref, held = refs
    for core, p, piece in gathered(me, refs, held):
        cols = piece.shape[1]
        size = piece.shape[0] // 4
        at = slice(p * size, (p + 1) * size)
        for t in range(4):
            start = core * cols + (2 * t * cols if t < 3 else 0)
            part = piece[t * size : (t + 1) * size].astype(f32)
            (qkv_ref if t < 3 else out_ref)[at, start : start + cols] = part


def place_vec_kernel(me, a_ref, b_ref, c_ref, d_ref, *outs):
    total = (a_ref[...] + b_ref[...]) + (c_ref[...] + d_ref[...])
    cut = total.shape[1] // 4
    for z in range(4):
        @pl.when(me[3] == z)
        def _():
            for i in range(8):
                outs[i][...] = total[i : i + 1, z * cut : (z + 1) * cut]
            outs[8][...] = total[8 + z : 9 + z]


def place_vec(me, parts):
    width = parts[0].shape[1]
    outs = [shape(1, width // 4, dtype=f32)] * 8 + [shape(1, width, dtype=f32)]
    return call(
        place_vec_kernel, (1,), [whole(a) for a in parts], outs,
        [whole(o) for o in outs], [], me, *parts, micros=1, mib=16,
    )


def place(me, kernel, outs, parts):
    outs = [shape(*dims, dtype=f32) for dims in outs]
    rows, cols = parts[0].shape
    return call(
        kernel, (1,), [whole(a) for a in parts], outs, [whole(o) for o in outs],
        [pltpu.VMEM((2, 2, 2, rows, cols), bf16)], me, *parts, micros=3, mib=16,
    )


def local(
    dp, seq, tokens, lengths, head_swap, w_qkv, bias_q, bias_v, w_out, bias_out, gain_attn,
    shift_attn, w_up, bias_up, w_down, bias_down, gain_ffn, shift_ffn, cotangent,
):
    seqs_here, part_len, width = tokens.shape
    heads = head_swap.shape[0]
    head_dim = width // heads
    rows = seqs_here * part_len
    assert seqs_here == 2 and seq == 4 and dp % 8 == 0
    spot = lax.axis_index("dp")
    z = lax.axis_index("seq")
    core = spot & 1
    odd = z & 1
    me = jnp.stack([core, (spot >> 1) & 1, (spot >> 2) & 1, z]).astype(jnp.int32)

    def over_dp(arr, bit):
        return lax.ppermute(arr, "dp", [(i, i ^ bit) for i in range(dp)])

    def over_seq(arr, bit):
        return lax.ppermute(arr, "seq", [(i, i ^ bit) for i in range(seq)])

    def other(arr):
        return over_dp(arr, 1)

    def tie(value, *others):
        return lax.optimization_barrier((value, others))[0]

    def there(i, r):
        d, k = divmod(i, seq)
        return ((d & ~1) | (k >> 1)) * seq + 2 * (d & 1) + (r ^ (k & 1))

    ways = [[(i, there(i, r)) for i in range(dp * seq)] for r in range(2)]

    def send_block(parts):
        out = []
        for r, part in enumerate(parts):
            out.append(lax.ppermute(part, ("dp", "seq"), ways[r]))
        return out

    def gather_block(arr):
        return send_block([lax.dynamic_index_in_dim(arr, r ^ odd, 0, False) for r in range(2)])

    def return_block(arr):
        back = []
        for r in range(2):
            part = arr[r * part_len : (r + 1) * part_len]
            back.append(lax.ppermute(part, ("dp", "seq"), [(b, a) for a, b in ways[r]]))
        return back

    def in_order(back):
        return jnp.where(odd_z, jnp.stack(back[::-1]), jnp.stack(back))

    near = gather_block(tokens)
    length = lax.ppermute(lax.dynamic_slice_in_dim(lengths, odd, 1, 0), ("dp", "seq"), ways[0])[0]

    def limit(block, half):
        return length - (block * rows + (half ^ odd) * part_len)

    info = jnp.concatenate(
        [
            jnp.stack([limit(core, 0), limit(core, 1), limit(1 - core, 0), limit(1 - core, 1)]),
            head_swap,
        ]
    ).astype(jnp.int32)
    far_flag = jnp.repeat(head_swap, head_dim)[None, :]
    biases = jnp.stack([bias_q, jnp.zeros_like(bias_q), bias_v])[:, None]
    given = [lax.dynamic_index_in_dim(cotangent, r ^ odd, 0, False) for r in range(2)]
    near, info, far_flag, biases, me, second, odd_z, given = tie(
        (near, info, far_flag, biases, me, core == 1, odd == 1, given)
    )
    far = far_flag == 1
    x = jnp.concatenate(near, 0)
    x_far = other(x)
    grad = send_block(tie(given, x))

    w_hbm = pltpu.with_memory_space_constraint(w_qkv, pltpu.HBM)
    q, k, v = qkv(info, x, x_far, w_hbm, far_flag, biases)
    ctx, probs = attn_fwd(info, q, k, v)
    probs = pltpu.with_memory_space_constraint(probs, pltpu.HBM)
    ctx_far = other(ctx)
    y, normed, rstd, act_m, act_t, slope_m, slope_t, out, d_two, d_ffn, vec_two = mid(
        me, x, ctx, w_out, bias_out[None], gain_attn[None], shift_attn[None], w_up, bias_up[None],
        w_down, bias_down[None], gain_ffn[None], shift_ffn[None], *grad,
    )

    def add(a, b):
        return (a.astype(f32) + b.astype(f32)).astype(bf16)

    def halve_first(stored):
        a_keep, a_send, b_keep, b_send = stored
        a, b = over_dp(a_send, 2), over_dp(b_send, 4)
        return add(a_keep, a), add(b_keep, b)

    def halve_second(pair):
        a, b = pair
        a_got, b_got = over_dp(a[1], 4), over_dp(b[1], 2)
        return jnp.stack([add(a[0], a_got), add(b[0], b_got)], 2)

    def halve_seq_first(c):
        got = over_seq(c[1], 1)
        return add(c[0], got)

    def halve_seq_second(kept, got):
        c = add(kept, got)
        bit = 8
        while bit < dp:
            c = add(c, over_dp(c, bit))
            bit *= 2
        return c

    def collect(c, *others):
        c = c.reshape(-1, c.shape[-1])
        own = [c] + [over_dp(c, bit) for bit in (4, 2, 6)]
        if others:
            own = tie(own, *others)
        return own + [other(o) for o in own]

    half = width // 2
    d_ffn_far = other(d_ffn)
    act_far = other(act_t)
    y_far = other(y)
    pre_m, pre_t, vec_up = back_one(me, d_ffn, w_down, slope_m, slope_t)
    pre_far = other(pre_t)
    output = return_block(tie(out, pre_m))
    down = grad_down(me, d_ffn, d_ffn_far, act_m, act_far)
    pre_m, down = tie((pre_m, down))
    down = halve_first(down)
    d_one, d_attn, d_ctx, vec_one = back_two(
        me, pre_m, pre_t, w_up, d_two, normed, rstd, gain_attn[None], w_out
    )

    def mine(pair):
        return jnp.where(second, pair[1], pair[0])

    attn_far = other(jnp.where(second, d_attn[:, :half], d_attn[:, half:]))
    y, d_ctx = tie((y, d_ctx))
    up = grad_up(me, y, y_far, pre_m, pre_far)
    d_ctx, up, down = tie((d_ctx, up, down))
    up = halve_first(up)
    down = halve_second(down)
    heads_far = [far[:, :half], far[:, half:]]
    pairs = heads // 4
    qs, ks, vs, k_gots, v_gots, vecs = [], [], [], [], [], []
    for i in range(2):
        d_q, d_k, d_v, vec = attn_bwd(info, i * pairs, pairs, q, k, v, d_ctx, ctx, probs)
        qs.append(d_q)
        ks.append(d_k)
        vs.append(d_v)
        vecs.append(vec)
        k_gots.append(other(d_k))
        v_gots.append(other(d_v))
    q_far = other(jnp.where(second, qs[0], qs[1]))
    k_own = [jnp.where(f, g, u) for f, g, u in zip(heads_far, k_gots, ks)]
    k_oth = [jnp.where(f, u, g) for f, g, u in zip(heads_far, k_gots, ks)]
    v_own = [jnp.where(f, g, u) for f, g, u in zip(heads_far, v_gots, vs)]
    v_oth = [jnp.where(f, u, g) for f, g, u in zip(heads_far, v_gots, vs)]

    rest = grad_rest(
        me, x, x_far, ctx, ctx_far, mine(qs), q_far, mine(k_own), mine(k_oth), mine(v_own),
        mine(v_oth), mine((d_attn[:, :half], d_attn[:, half:])), attn_far,
    )
    rest, qs, vecs, down, up = tie((rest, qs, vecs, down, up))
    rest = halve_first(rest)
    up = halve_second(up)
    down = halve_seq_first(down)
    d_tok = tok(me, qs + k_own + v_own, w_qkv, d_one)
    d_tok = return_block(d_tok)
    vec = jnp.concatenate(
        [jnp.concatenate(vecs, 1), vec_one, vec_two, vec_up], 0
    )
    vec = vec + other(vec)
    bit = 8
    while bit < dp:
        vec = vec + over_dp(vec, bit)
        bit *= 2
    v_got = [over_dp(vec, bit) for bit in (4, 2, 6)]
    down_got = over_seq(down[1], 2)
    up = halve_seq_first(up)
    rest = halve_second(rest)
    v_y, v_x, v_d = v_got
    rest = halve_seq_first(rest)
    up = halve_seq_second(up[0], over_seq(up[1], 2))
    down = halve_seq_second(down[0], down_got)
    (s_down,) = place(me, place_down_kernel, [(width, width)], collect(down))
    vec = (vec + v_y) + (v_x + v_d)
    vec_z = [vec] + [over_seq(vec, bit) for bit in (1, 2, 3)]
    rest = halve_seq_second(rest[0], over_seq(rest[1], 2))
    (s_up,) = place(me, place_up_kernel, [(width // seq, w_up.shape[1])], collect(up))
    d_tokens = in_order(d_tok).astype(f32)
    vec = place_vec(me, vec_z)
    rest = collect(rest)
    s_qkv, s_out = place(
        me, place_rest_kernel, [(width // seq, 3 * width), (width // seq, width)], rest
    )
    output = in_order(output)
    s_bq, s_bv, s_ga, s_sa, s_bo, s_gf, s_sf, s_bd, s_b_up = (
        v.reshape(-1) for v in vec
    )
    return (
        output, d_tokens, s_qkv, s_bq, s_bv, s_out, s_bo, s_ga, s_sa, s_up, s_b_up, s_down, s_bd,
        s_gf, s_sf,
    )


def solution(mesh):
    dp, seq = mesh.shape["dp"], mesh.shape["seq"]
    rows = P("dp", "seq", None)
    placed = (rows, P("dp")) + (P(),) * 14 + (rows,)
    cut, line = P("seq", None), P("seq")

    def body(*args):
        return local(dp, seq, *args)

    return jax.shard_map(
        body,
        mesh=mesh,
        in_specs=placed,
        out_specs=(
            rows, rows, cut, line, line, cut, line, line, line, cut, line, cut, line, line, line,
        ),
        check_vma=False,
    )
```

```python
import functools

import jax
import jax.numpy as jnp
from jax import lax
from jax.experimental import pallas as pl
from jax.experimental.pallas import tpu as pltpu
from jax.sharding import PartitionSpec as P


f32 = jnp.float32
bf16 = jnp.bfloat16
NN = (((1,), (0,)), ((), ()))
NT = (((1,), (1,)), ((), ()))
TN = (((0,), (0,)), ((), ()))

CHUNK = 256


def mm(a, b, dims=NN):
    return lax.dot_general(a, b, dims, preferred_element_type=f32)


def shape(*dims, dtype=bf16):
    return jax.ShapeDtypeStruct(dims, dtype)


def whole(arr):
    zeros = (0,) * arr.ndim
    return pl.BlockSpec(arr.shape, lambda *_: zeros)


def call(kernel, grid, specs, outs, out_specs, scratch, scalars, *args, micros=8, mib=16):
    return pl.pallas_call(
        kernel,
        grid_spec=pltpu.PrefetchScalarGridSpec(
            num_scalar_prefetch=1,
            grid=grid,
            in_specs=specs,
            out_specs=out_specs,
            scratch_shapes=scratch,
        ),
        out_shape=outs,
        cost_estimate=pl.CostEstimate(
            flops=micros * 1_000_000_000, bytes_accessed=8_000_000, transcendentals=0
        ),
        compiler_params=pltpu.CompilerParams(vmem_limit_bytes=mib << 20),
    )(scalars, *args)


def limits(info, pair, h, place, half):
    swap = info[4 + 2 * pair + h]
    first = jnp.where(swap == 1, info[2], info[0])
    second = jnp.where(swap == 1, info[3], info[1])
    return place < jnp.where(place < half, first, second + half)


def qkv_kernel(info, x_ref, xf_ref, w_ref, far_ref, bias_ref, q_ref, k_ref, v_ref, near):
    t = pl.program_id(0)
    near[...] = mm(x_ref[...], w_ref[...])

    @pl.when(t == 0)
    def _():
        scale = bf16((q_ref.shape[1] // (info.shape[0] - 4)) ** -0.5)
        q_ref[...] = (near[...] + bias_ref[0]).astype(bf16) * scale

    @pl.when(t > 0)
    def _():
        picked = jnp.where(far_ref[...] == 1, mm(xf_ref[...], w_ref[...]), near[...])
        picked = (picked + bias_ref[0]).astype(bf16)
        for i, out_ref in ((1, k_ref), (2, v_ref)):
            @pl.when(t == i)
            def _():
                out_ref[...] = picked


def qkv(info, x, x_far, w, far, bias):
    rows, width = x.shape
    full = pl.BlockSpec((rows, width), lambda j, s: (0, 0))
    return call(
        qkv_kernel, (3,),
        [full, full, pl.BlockSpec((width, width), lambda j, s: (0, j)), whole(far),
         pl.BlockSpec((1, 1, width), lambda j, s: (j, 0, 0))],
        [shape(rows, width)] * 3, [full] * 3, [pltpu.VMEM((rows, width), f32)],
        info, x, x_far, w, far, bias, micros=5,
    )


def attn_fwd_kernel(info, q_ref, k_ref, v_ref, ctx_ref, p_ref):
    rows = q_ref.shape[0]
    lanes = 128
    hd = lanes // 2
    lane = lax.broadcasted_iota(jnp.int32, (rows, lanes), 1)
    place = lax.broadcasted_iota(jnp.int32, (rows, rows), 0)
    count = q_ref.shape[1] // lanes
    for i in range(count):
        cols = slice(i * lanes, (i + 1) * lanes)
        q = q_ref[:, cols]
        k = k_ref[:, cols]
        v = v_ref[:, cols]
        parts = []
        for h in range(2):
            mine = (lane < hd) if h == 0 else (lane >= hd)
            s = mm(jnp.where(mine, k, jnp.zeros_like(k)), q, NT)
            ok = limits(info, pl.program_id(0) * count + i, h, place, rows // 2)
            s = jnp.where(ok, s, f32(-10000.0))
            e = jnp.exp(s - jnp.max(s, 0, keepdims=True))
            p = (e * (1.0 / jnp.sum(e, 0, keepdims=True))).astype(bf16)
            p_ref[2 * i + h] = p
            parts.append(mm(p, v, TN))
        ctx_ref[:, cols] = jnp.where(lane < hd, parts[0], parts[1]).astype(bf16)


def attn_fwd(info, q, k, v):
    rows, width = q.shape
    pairs = width // 128
    blk = pl.BlockSpec((rows, 256), lambda j, s: (0, j))
    sq = pl.BlockSpec((4, rows, rows), lambda j, s: (j, 0, 0))
    return call(
        attn_fwd_kernel, (pairs // 2,), [blk] * 3,
        [shape(rows, width), pltpu.HBM((2 * pairs, rows, rows), bf16)], [blk, sq], [], info, q, k, v,
    )


def attn_bwd_kernel(
    start, info, q_ref, k_ref, v_ref, g_ref, c_ref, p_ref, dq_ref, dk_ref, dv_ref, vec_ref
):
    pair = pl.program_id(0) + start
    rows, lanes = q_ref.shape
    hd = lanes // 2
    lane = lax.broadcasted_iota(jnp.int32, (rows, lanes), 1)
    place = lax.broadcasted_iota(jnp.int32, (rows, lanes), 0)
    q = q_ref[...]
    k = k_ref[...]
    v = v_ref[...]
    g = g_ref[...]
    zero = jnp.zeros_like(k)
    oks = [limits(info, pair, h, place, rows // 2) for h in range(2)]
    ok = jnp.where(lane < hd, jnp.where(oks[0], 1, 0), jnp.where(oks[1], 1, 0)) == 1
    kt = jnp.transpose(jnp.where(ok, k, zero))
    dvs, dks, dqs = [], [], []
    prod = jnp.transpose(g.astype(f32) * c_ref[...].astype(f32))
    for h in range(2):
        mine = (lane < hd) if h == 0 else (lane >= hd)
        dp = mm(jnp.where(mine, v, zero), g, NT)
        pb = p_ref[h]
        p = pb.astype(f32)
        inner = jnp.sum(prod[h * hd : (h + 1) * hd], 0, keepdims=True)
        ds = (p * (dp - inner)).astype(bf16)
        dvs.append(mm(pb, g))
        dks.append(mm(ds, q))
        dqs.append(mm(kt[h * hd : (h + 1) * hd], ds))
    dv = jnp.where(lane < hd, dvs[0], dvs[1]).astype(bf16)
    dq = (jnp.transpose(jnp.concatenate(dqs, 0)) * f32(hd**-0.5)).astype(bf16)
    dv_ref[...] = dv
    dk_ref[...] = jnp.where(ok, jnp.where(lane < hd, dks[0], dks[1]), f32(0.0)).astype(bf16)
    dq_ref[...] = dq
    vec_ref[0:1] = jnp.sum(dq.astype(f32), 0, keepdims=True)
    vec_ref[1:2] = jnp.sum(dv.astype(f32), 0, keepdims=True)


def attn_bwd(info, first, pairs, q, k, v, g, c, p):
    rows = q.shape[0]
    blk = pl.BlockSpec((rows, 128), lambda j, s: (0, j + first))
    sq = pl.BlockSpec((2, rows, rows), lambda j, s: (j + first, 0, 0))
    out = pl.BlockSpec((rows, 128), lambda j, s: (0, j))
    return call(
        functools.partial(attn_bwd_kernel, first), (pairs,), [blk] * 5 + [sq],
        [shape(rows, 128 * pairs)] * 3 + [shape(2, 128 * pairs, dtype=f32)],
        [out] * 3 + [pl.BlockSpec((2, 128), lambda j, s: (0, j))],
        [], info, q, k, v, g, c, p, micros=6, mib=16,
    )


def normalize(hidden):
    center = hidden - jnp.mean(hidden, -1, keepdims=True)
    rstd = lax.rsqrt(jnp.mean(center * center, -1, keepdims=True) + 1e-05)
    return center * rstd, rstd


def norm_back(scaled, normed, rstd):
    return rstd * (
        scaled
        - jnp.mean(scaled, -1, keepdims=True)
        - normed * jnp.mean(scaled * normed, -1, keepdims=True)
    )


def by_rows(rows, size, body):
    def step(i, carry):
        body(pl.ds(pl.multiple_of(i * size, size), size))
        return carry

    lax.fori_loop(0, rows // size, step, 0)


def gelu_both(x):
    t = 1.0 / (1.0 + f32(0.3275911 * 0.7071067811865476) * jnp.abs(x))
    poly = f32(-1.453152027 / 2) + t * f32(1.061405429 / 2)
    poly = f32(1.421413741 / 2) + t * poly
    poly = f32(-0.284496736 / 2) + t * poly
    poly = t * (f32(0.254829592 / 2) + t * poly)
    bell = jnp.exp(x * x * f32(-0.5))
    tail = poly * bell
    dist = jnp.where(x >= 0, 1.0 - tail, tail)
    return x * dist, dist + x * bell * f32(0.3989422804014327)


def quarters(array, axis, cut):
    specs = []
    for far in range(2):
        for k in range(2):
            def index(j, s, far=far, k=k):
                at = 2 * (2 * j + k) + (s[0] ^ far)
                return (at, 0) if axis == 0 else (0, at)

            dims = list(array.shape)
            dims[axis] = cut
            specs.append(pl.BlockSpec(tuple(dims), index))
    return specs


def mid_kernel(
    me, x_ref, ctx_ref, wo_ref, bo_ref, ga_ref, sa_ref, wu0, wu1, wu2, wu3, bu0, bu1, bu2, bu3,
    wd0, wd1, wd2, wd3, bd_ref, gf_ref, sf_ref, g0_ref, g1_ref,
    y_ref, n_ref, r_ref, am_ref, at_ref, dm_ref, dt_ref, out0, out1, dtwo_ref, dffn_ref, vec_ref,
    acc, grad,
):
    j = pl.program_id(0)
    rows = x_ref.shape[0]
    part_len = rows // 2

    @pl.when(j == 0)
    def _():
        acc[...] = mm(ctx_ref[...], wo_ref[...])

        def first(at):
            normed, rstd = normalize(x_ref[at].astype(f32) + (acc[at] + bo_ref[...]))
            n_ref[at] = normed
            r_ref[at] = rstd
            y_ref[at] = (normed * ga_ref[...] + sa_ref[...]).astype(bf16)

        by_rows(rows, CHUNK, first)

    y = y_ref[...]
    part = None
    for wus, bus, wds, a_ref, d_ref in (
        ((wu0, wu1), (bu0, bu1), (wd0, wd1), am_ref, dm_ref),
        ((wu2, wu3), (bu2, bu3), (wd2, wd3), at_ref, dt_ref),
    ):
        up = jnp.concatenate([w[...] for w in wus], 1)
        pre = mm(y, up) + jnp.concatenate([b[...] for b in bus], 1)
        act, slope = gelu_both(pre)
        act = act.astype(bf16)
        a_ref[...] = act
        d_ref[...] = slope.astype(bf16)
        more = mm(act, jnp.concatenate([w[...] for w in wds], 0))
        part = more if part is None else part + more

    @pl.when(j == 0)
    def _():
        acc[...] = part

    @pl.when(j == 1)
    def _():
        acc[...] += part
        vec_ref[...] = jnp.zeros_like(vec_ref)
        grad[:part_len] = g0_ref[...]
        grad[part_len:] = g1_ref[...]

        def second(at):
            normed, rstd = normalize(y_ref[at].astype(f32) + (acc[at] + bd_ref[...]))
            out = (normed * gf_ref[...] + sf_ref[...]).astype(bf16)
            for k, out_ref in ((0, out0), (1, out1)):
                @pl.when(at.start == k * part_len)
                def _():
                    out_ref[...] = out

            g = grad[at].astype(f32)
            d_two = norm_back(g * gf_ref[...], normed, rstd)
            dtwo_ref[at] = d_two
            d_ffn = d_two.astype(bf16)
            dffn_ref[at] = d_ffn
            vec_ref[0:1] += jnp.sum(g * normed, 0, keepdims=True)
            vec_ref[1:2] += jnp.sum(g, 0, keepdims=True)
            vec_ref[2:3] += jnp.sum(d_ffn.astype(f32), 0, keepdims=True)

        by_rows(rows, part_len, second)


def mid(me, x, ctx, wo, bo, ga, sa, wu, bu, wd, bd, gf, sf, g0, g1):
    rows, width = x.shape
    ff = wu.shape[1]
    cut = ff // 8
    full = pl.BlockSpec((rows, width), lambda j, s: (0, 0))
    col = pl.BlockSpec((rows, 2 * cut), lambda j, s: (0, j))
    vec = shape(3, width, dtype=f32)
    rstd = shape(rows, 1, dtype=f32)
    return call(
        mid_kernel, (2,),
        [full, full, whole(wo), whole(bo), whole(ga), whole(sa)] + quarters(wu, 1, cut)
        + quarters(bu, 1, cut) + quarters(wd, 0, cut) + [whole(bd), whole(gf), whole(sf), whole(g0), whole(g1)],
        [shape(rows, width), shape(rows, width, dtype=f32), rstd] + [shape(rows, ff // 2)] * 4
        + [shape(rows // 2, width)] * 2
        + [shape(rows, width, dtype=f32), shape(rows, width), vec],
        [full, full, whole(rstd)] + [col] * 4 + [whole(g0)] * 2 + [full, full, whole(vec)],
        [pltpu.VMEM((rows, width), f32), pltpu.VMEM((rows, width), bf16)],
        me, x, ctx, wo, bo, ga, sa, *[wu] * 4, *[bu] * 4, *[wd] * 4, bd, gf, sf, g0, g1,
        micros=18, mib=26,
    )


def back_one_kernel(me, dffn_ref, wd0, wd1, wd2, wd3, dm_ref, dt_ref, pm_ref, pt_ref, vec_ref):
    j = pl.program_id(0)
    d_ffn = dffn_ref[...]
    cut = wd0.shape[0]
    for far, wds, d_ref, p_ref in (
        (0, (wd0, wd1), dm_ref, pm_ref), (1, (wd2, wd3), dt_ref, pt_ref),
    ):
        down = jnp.concatenate([w[...] for w in wds], 0)
        d_pre = (mm(d_ffn, down, NT) * d_ref[...].astype(f32)).astype(bf16)
        p_ref[...] = d_pre
        total = jnp.sum(d_pre.astype(f32), 0, keepdims=True)
        span = pl.ds(pl.multiple_of((me[0] ^ far) * cut, cut), cut)
        for k in range(2):
            vec_ref[pl.ds(2 * j + k, 1), span] = total[:, k * cut : (k + 1) * cut]


def back_one(me, dffn, wd, dm, dt):
    rows, width = dffn.shape
    ff = wd.shape[0]
    cut = ff // 8
    full = pl.BlockSpec((rows, width), lambda j, s: (0, 0))
    col = pl.BlockSpec((rows, 2 * cut), lambda j, s: (0, j))
    vec = shape(4, 2 * cut, dtype=f32)
    return call(
        back_one_kernel, (2,), [full] + quarters(wd, 0, cut) + [col, col],
        [shape(rows, ff // 2), shape(rows, ff // 2), vec], [col, col, whole(vec)],
        [], me, dffn, *[wd] * 4, dm, dt, micros=6,
    )


def back_two_kernel(
    me, pm_ref, pt_ref, wu0, wu1, wu2, wu3, dtwo_ref, n_ref, r_ref, gain_ref, wo_ref,
    done_ref, dattn_ref, dctx_ref, vec_ref, acc,
):
    j = pl.program_id(0)
    part = mm(pm_ref[...], jnp.concatenate([wu0[...], wu1[...]], 1), NT)
    part = part + mm(pt_ref[...], jnp.concatenate([wu2[...], wu3[...]], 1), NT)

    @pl.when(j == 0)
    def _():
        acc[...] = part

    @pl.when(j == 1)
    def _():
        acc[...] += part
        rows = acc.shape[0]
        vec_ref[...] = jnp.zeros_like(vec_ref)

        def last(at):
            d_y = acc[at] + dtwo_ref[at]
            normed = n_ref[at]
            d_one = norm_back(d_y * gain_ref[...], normed, r_ref[at])
            done_ref[at] = d_one
            d_attn = d_one.astype(bf16)
            dattn_ref[at] = d_attn
            vec_ref[0:1] += jnp.sum(d_y * normed, 0, keepdims=True)
            vec_ref[1:2] += jnp.sum(d_y, 0, keepdims=True)
            vec_ref[2:3] += jnp.sum(d_attn.astype(f32), 0, keepdims=True)

        by_rows(rows, CHUNK, last)
        dctx_ref[...] = mm(dattn_ref[...], wo_ref[...], NT).astype(bf16)


def back_two(me, pm, pt, wu, dtwo, n, r, gain, wo):
    rows, width = dtwo.shape
    ff = wu.shape[1]
    cut = ff // 8
    full = pl.BlockSpec((rows, width), lambda j, s: (0, 0))
    col = pl.BlockSpec((rows, 2 * cut), lambda j, s: (0, j))
    vec = shape(3, width, dtype=f32)
    return call(
        back_two_kernel, (2,),
        [col, col] + quarters(wu, 1, cut) + [full, full, whole(r), whole(gain), whole(wo)],
        [shape(rows, width, dtype=f32), shape(rows, width), shape(rows, width), vec],
        [full, full, full, whole(vec)],
        [pltpu.VMEM((rows, width), f32)],
        me, pm, pt, *[wu] * 4, dtwo, n, r, gain, wo, micros=8,
    )


def transposed(left, first, second):
    rows = first.shape[0]

    @pl.when(pl.program_id(0) == 0)
    def _():
        left[:, :rows] = jnp.transpose(first[...])
        left[:, rows:] = jnp.transpose(second[...])

    return left[:, :rows], left[:, rows:]


def grad_down_kernel(me, lo_ref, lp_ref, ro_ref, rp_ref, ak, asd, bk, bsd, left, tile):
    lo, lp = transposed(left, lo_ref, lp_ref)
    tile[...] = mm(lo, ro_ref[...]) + mm(lp, rp_ref[...])
    depth = tile.shape[0] // 4
    cols = tile.shape[1] // 2
    size = depth // 2
    for low in range(2):
        k0 = low ^ (me[3] & 1)
        across = slice(low * cols, (low + 1) * cols)
        for xr in range(2):
            for yr in range(2):
                at = pl.multiple_of((2 * (xr ^ me[1]) + (yr ^ me[2])) * depth, size)
                (asd if xr else ak)[yr, k0, 0] = tile[pl.ds(at, size), across].astype(bf16)
                at = pl.multiple_of(at + size, size)
                (bsd if yr else bk)[xr, k0, 0] = tile[pl.ds(at, size), across].astype(bf16)


def grad_down(me, lo, lp, ro, rp):
    rows, width = lo.shape
    cut = ro.shape[1] // 2
    size = width // 8
    full = pl.BlockSpec((rows, width), lambda j, s: (0, 0))
    col = pl.BlockSpec((rows, cut), lambda j, s: (0, j ^ (s[3] >> 1)))
    out = pl.BlockSpec((2, 2, 1, size, cut // 2), lambda j, s: (0, 0, j, 0, 0))
    return call(
        grad_down_kernel, (2,), [full, full, col, col],
        [shape(2, 2, 2, size, cut // 2)] * 4, [out] * 4,
        [pltpu.VMEM((width, 2 * rows), bf16), pltpu.VMEM((width, cut), f32)],
        me, lo, lp, ro, rp, micros=6,
    )


def grad_up_kernel(me, lo_ref, lp_ref, ro_ref, rp_ref, ak, asd, bk, bsd, left, tile):
    lo, lp = transposed(left, lo_ref, lp_ref)
    tile[...] = mm(lo, ro_ref[...]) + mm(lp, rp_ref[...])
    depth = tile.shape[0] // 4
    cols = tile.shape[1] // 2
    size = depth // 2

    def store(a_ref):
        for yr in range(2):
            across = pl.ds(pl.multiple_of((yr ^ me[2]) * cols, 128), cols)
            for zr in range(4):
                at = pl.multiple_of((zr ^ me[3]) * depth, size)
                a_ref[yr, zr & 1, zr >> 1] = tile[pl.ds(at, size), across].astype(bf16)
                at = pl.multiple_of(at + size, size)
                (bsd if yr else bk)[0, zr & 1, zr >> 1] = tile[pl.ds(at, size), across].astype(bf16)

    pl.when(pl.program_id(0) == 0)(lambda: store(ak))
    pl.when(pl.program_id(0) == 1)(lambda: store(asd))


def grad_up(me, lo, lp, ro, rp):
    rows, width = lo.shape
    cut = ro.shape[1] // 2
    size = width // 8
    full = pl.BlockSpec((rows, width), lambda j, s: (0, 0))
    col = pl.BlockSpec((rows, cut), lambda j, s: (0, j ^ s[1]))
    a_out = pl.BlockSpec((2, 2, 2, size, cut // 2), lambda j, s: (0, 0, 0, 0, 0))
    b_out = pl.BlockSpec((1, 2, 2, size, cut // 2), lambda j, s: (j, 0, 0, 0, 0))
    return call(
        grad_up_kernel, (2,), [full, full, col, col],
        [shape(2, 2, 2, size, cut // 2)] * 4, [a_out, a_out, b_out, b_out],
        [pltpu.VMEM((width, 2 * rows), bf16), pltpu.VMEM((width, cut), f32)],
        me, lo, lp, ro, rp, micros=6,
    )


def grad_rest_kernel(
    me, xo_ref, xp_ref, co_ref, cp_ref, qo_ref, qp_ref, ko_ref, kp_ref, vo_ref, vp_ref, ao_ref, ap_ref,
    ak, asd, bk, bsd, left, tile,
):
    rows = xo_ref.shape[0]
    deep = tile.shape[0] // 4
    size = deep // 4
    for t, (own, other) in enumerate(
        ((qo_ref, qp_ref), (ko_ref, kp_ref), (vo_ref, vp_ref), (ao_ref, ap_ref))
    ):
        if t in (0, 3):
            first, second = (co_ref, cp_ref) if t == 3 else (xo_ref, xp_ref)
            left[:, :rows] = jnp.transpose(first[...])
            left[:, rows:] = jnp.transpose(second[...])
        tile[...] = mm(left[:, :rows], own[...]) + mm(left[:, rows:], other[...])
        put = slice((t % 2) * size, (t % 2 + 1) * size)
        for xr in range(2):
            for yr in range(2):
                for zr in range(4):
                    at = (zr ^ me[3]) * deep + (2 * (xr ^ me[1]) + (yr ^ me[2])) * size
                    piece = tile[pl.ds(pl.multiple_of(at, size), size), :].astype(bf16)
                    if t < 2:
                        (asd if xr else ak)[yr, zr & 1, zr >> 1, put] = piece
                    else:
                        (bsd if yr else bk)[xr, zr & 1, zr >> 1, put] = piece


def grad_rest(me, *args):
    rows, width = args[0].shape
    half = width // 2
    dims = (2, 2, 2, width // 8, half)
    return call(
        grad_rest_kernel, (1,), [whole(a) for a in args], [shape(*dims)] * 4,
        [pl.BlockSpec(dims, lambda j, s: (0,) * 5)] * 4,
        [pltpu.VMEM((width, 2 * rows), bf16), pltpu.VMEM((width, half), f32)],
        me, *args, micros=6,
    )


def tok_kernel(me, q0, q1, k0, k1, v0, v1, wq_ref, wk_ref, wv_ref, done_ref, out0, out1):
    total = done_ref[...]
    for first, second, w_ref in ((q0, q1, wq_ref), (k0, k1, wk_ref), (v0, v1, wv_ref)):
        total = total + mm(jnp.concatenate([first[...], second[...]], 1), w_ref[...], NT)
    total = total.astype(bf16)
    half = out0.shape[0]
    out0[...] = total[:half]
    out1[...] = total[half:]


def tok(me, parts, w, done):
    rows, width = done.shape
    thirds = [pl.BlockSpec((width, width), lambda j, s, t=t: (0, t)) for t in range(3)]
    return call(
        tok_kernel, (1,), [whole(a) for a in parts] + thirds + [whole(done)],
        [shape(rows // 2, width)] * 2, [pl.BlockSpec((rows // 2, width), lambda j, s: (0, 0))] * 2, [],
        me, *parts, w, w, w, done, micros=5,
    )


def gathered(me, refs, held):
    for core in range(2):
        for xr in range(2):
            for yr in range(2):
                held[core ^ me[0], xr ^ me[1], yr ^ me[2]] = refs[4 * core + 2 * xr + yr][...]
    return [(core, p, held[core, p >> 1, p & 1]) for core in range(2) for p in range(4)]


def place_down_kernel(me, *refs):
    *refs, out_ref, held = refs
    for core, p, piece in gathered(me, refs, held):
        rows, cols = piece.shape
        at = slice(core * cols, (core + 1) * cols)
        out_ref[at, p * rows : (p + 1) * rows] = jnp.transpose(piece.astype(f32))


def place_up_kernel(me, *refs):
    *refs, out_ref, held = refs
    for core, p, piece in gathered(me, refs, held):
        cols = piece.shape[1]
        start = (2 * p + core) * cols
        out_ref[:, start : start + cols] = piece.astype(f32)


def place_rest_kernel(me, *refs):
    *refs, qkv_ref, out_ref, held = refs
    for core, p, piece in gathered(me, refs, held):
        cols = piece.shape[1]
        size = piece.shape[0] // 4
        at = slice(p * size, (p + 1) * size)
        for t in range(4):
            start = core * cols + (2 * t * cols if t < 3 else 0)
            part = piece[t * size : (t + 1) * size].astype(f32)
            (qkv_ref if t < 3 else out_ref)[at, start : start + cols] = part


def place_vec_kernel(me, a_ref, b_ref, c_ref, d_ref, *outs):
    total = (a_ref[...] + b_ref[...]) + (c_ref[...] + d_ref[...])
    cut = total.shape[1] // 4
    for z in range(4):
        @pl.when(me[3] == z)
        def _():
            for i in range(8):
                outs[i][...] = total[i : i + 1, z * cut : (z + 1) * cut]
            outs[8][...] = total[8 + z : 9 + z]


def place_vec(me, parts):
    width = parts[0].shape[1]
    outs = [shape(1, width // 4, dtype=f32)] * 8 + [shape(1, width, dtype=f32)]
    return call(
        place_vec_kernel, (1,), [whole(a) for a in parts], outs,
        [whole(o) for o in outs], [], me, *parts, micros=1, mib=16,
    )


def place(me, kernel, outs, parts):
    outs = [shape(*dims, dtype=f32) for dims in outs]
    rows, cols = parts[0].shape
    return call(
        kernel, (1,), [whole(a) for a in parts], outs, [whole(o) for o in outs],
        [pltpu.VMEM((2, 2, 2, rows, cols), bf16)], me, *parts, micros=3, mib=16,
    )


def local(
    dp, seq, tokens, lengths, head_swap, w_qkv, bias_q, bias_v, w_out, bias_out, gain_attn,
    shift_attn, w_up, bias_up, w_down, bias_down, gain_ffn, shift_ffn, cotangent,
):
    seqs_here, part_len, width = tokens.shape
    heads = head_swap.shape[0]
    head_dim = width // heads
    rows = seqs_here * part_len
    assert seqs_here == 2 and seq == 4 and dp % 8 == 0
    spot = lax.axis_index("dp")
    z = lax.axis_index("seq")
    core = spot & 1
    odd = z & 1
    me = jnp.stack([core, (spot >> 1) & 1, (spot >> 2) & 1, z]).astype(jnp.int32)

    def over_dp(arr, bit):
        return lax.ppermute(arr, "dp", [(i, i ^ bit) for i in range(dp)])

    def over_seq(arr, bit):
        return lax.ppermute(arr, "seq", [(i, i ^ bit) for i in range(seq)])

    def other(arr):
        return over_dp(arr, 1)

    def tie(value, *others):
        return lax.optimization_barrier((value, others))[0]

    def there(i, r):
        d, k = divmod(i, seq)
        return ((d & ~1) | (k >> 1)) * seq + 2 * (d & 1) + (r ^ (k & 1))

    ways = [[(i, there(i, r)) for i in range(dp * seq)] for r in range(2)]

    def send_block(parts):
        out = []
        for r, part in enumerate(parts):
            out.append(lax.ppermute(part, ("dp", "seq"), ways[r]))
        return out

    def gather_block(arr):
        return send_block([lax.dynamic_index_in_dim(arr, r ^ odd, 0, False) for r in range(2)])

    def return_block(parts):
        back = []
        for r, part in enumerate(parts):
            back.append(lax.ppermute(part, ("dp", "seq"), [(b, a) for a, b in ways[r]]))
        return back

    def in_order(back):
        return jnp.where(odd_z, jnp.stack(back[::-1]), jnp.stack(back))

    near = gather_block(tokens)
    length = lax.ppermute(lax.dynamic_slice_in_dim(lengths, odd, 1, 0), ("dp", "seq"), ways[0])[0]

    def limit(block, half):
        return length - (block * rows + (half ^ odd) * part_len)

    info = jnp.concatenate(
        [
            jnp.stack([limit(core, 0), limit(core, 1), limit(1 - core, 0), limit(1 - core, 1)]),
            head_swap,
        ]
    ).astype(jnp.int32)
    far_flag = jnp.repeat(head_swap, head_dim)[None, :]
    biases = jnp.stack([bias_q, jnp.zeros_like(bias_q), bias_v])[:, None]
    given = [lax.dynamic_index_in_dim(cotangent, r ^ odd, 0, False) for r in range(2)]
    near, info, far_flag, biases, me, second, odd_z, given = tie(
        (near, info, far_flag, biases, me, core == 1, odd == 1, given)
    )
    far = far_flag == 1
    x = jnp.concatenate(near, 0)
    x_far = other(x)
    grad = send_block(tie(given, x))

    w_hbm = pltpu.with_memory_space_constraint(w_qkv, pltpu.HBM)
    q, k, v = qkv(info, x, x_far, w_hbm, far_flag, biases)
    ctx, probs = attn_fwd(info, q, k, v)

    ctx_far = other(ctx)
    y, normed, rstd, act_m, act_t, slope_m, slope_t, out0, out1, d_two, d_ffn, vec_two = mid(
        me, x, ctx, w_out, bias_out[None], gain_attn[None], shift_attn[None], w_up, bias_up[None],
        w_down, bias_down[None], gain_ffn[None], shift_ffn[None], *grad,
    )

    def add(a, b):
        return (a.astype(f32) + b.astype(f32)).astype(bf16)

    def halve_first(stored):
        a_keep, a_send, b_keep, b_send = stored
        a, b = over_dp(a_send, 2), over_dp(b_send, 4)
        return add(a_keep, a), add(b_keep, b)

    def halve_second(pair):
        a, b = pair
        a_got, b_got = over_dp(a[1], 4), over_dp(b[1], 2)
        return jnp.stack([add(a[0], a_got), add(b[0], b_got)], 2)

    def halve_seq_first(c):
        got = over_seq(c[1], 1)
        return add(c[0], got)

    def halve_seq_second(kept, got):
        c = add(kept, got)
        bit = 8
        while bit < dp:
            c = add(c, over_dp(c, bit))
            bit *= 2
        return c

    def collect(c, *others):
        c = c.reshape(-1, c.shape[-1])
        own = [c] + [over_dp(c, bit) for bit in (4, 2, 6)]
        if others:
            own = tie(own, *others)
        return own + [other(o) for o in own]

    half = width // 2
    d_ffn_far = other(d_ffn)
    act_far = other(act_t)
    y_far = other(y)
    pre_m, pre_t, vec_up = back_one(me, d_ffn, w_down, slope_m, slope_t)
    pre_far = other(pre_t)
    output = return_block((out0, out1))
    down = grad_down(me, d_ffn, d_ffn_far, act_m, act_far)
    up = grad_up(me, y, y_far, pre_m, pre_far)
    down = halve_first(down)
    up = halve_first(up)
    d_one, d_attn, d_ctx, vec_one = back_two(
        me, pre_m, pre_t, w_up, d_two, normed, rstd, gain_attn[None], w_out
    )

    def mine(pair):
        return jnp.where(second, pair[1], pair[0])

    d_mine = (d_attn[:, :half], d_attn[:, half:])
    attn_far = other(mine(d_mine[::-1]))
    down = halve_second(down)
    up = halve_second(up)
    heads_far = [far[:, :half], far[:, half:]]
    pairs = heads // 4
    qs, ks, vs, k_gots, v_gots, vecs = [], [], [], [], [], []
    for i in range(2):
        d_q, d_k, d_v, vec = attn_bwd(info, i * pairs, pairs, q, k, v, d_ctx, ctx, probs)
        qs.append(d_q)
        ks.append(d_k)
        vs.append(d_v)
        vecs.append(vec)
        k_gots.append(other(d_k))
        v_gots.append(other(d_v))
    q_far = other(jnp.where(second, qs[0], qs[1]))
    down = halve_seq_first(down)
    k_own = [jnp.where(f, g, u) for f, g, u in zip(heads_far, k_gots, ks)]
    k_oth = [jnp.where(f, u, g) for f, g, u in zip(heads_far, k_gots, ks)]
    v_own = [jnp.where(f, g, u) for f, g, u in zip(heads_far, v_gots, vs)]
    v_oth = [jnp.where(f, u, g) for f, g, u in zip(heads_far, v_gots, vs)]

    rest = grad_rest(
        me, x, x_far, ctx, ctx_far, mine(qs), q_far, mine(k_own), mine(k_oth), mine(v_own),
        mine(v_oth), mine(d_mine), attn_far,
    )
    rest = halve_first(rest)
    d_tok = tok(me, qs + k_own + v_own, w_qkv, d_one)
    d_tok = return_block(d_tok)
    vec = jnp.concatenate(
        [jnp.concatenate(vecs, 1), vec_one, vec_two, vec_up], 0
    )
    vec = vec + other(vec)
    bit = 8
    while bit < dp:
        vec = vec + over_dp(vec, bit)
        bit *= 2
    v_got = [over_dp(vec, bit) for bit in (4, 2, 6)]
    down_got = over_seq(down[1], 2)
    up = halve_seq_first(up)
    rest = halve_second(rest)
    v_y, v_x, v_d = v_got
    rest = halve_seq_first(rest)
    up = halve_seq_second(up[0], over_seq(up[1], 2))
    down = halve_seq_second(down[0], down_got)
    (s_down,) = place(me, place_down_kernel, [(width, width)], collect(down))
    vec = (vec + v_y) + (v_x + v_d)
    vec_z = [vec] + [over_seq(vec, bit) for bit in (1, 2, 3)]
    rest = halve_seq_second(rest[0], over_seq(rest[1], 2))
    (s_up,) = place(me, place_up_kernel, [(width // seq, w_up.shape[1])], collect(up))
    d_tokens = in_order(d_tok).astype(f32)
    vec = place_vec(me, vec_z)
    rest = collect(rest)
    s_qkv, s_out = place(
        me, place_rest_kernel, [(width // seq, 3 * width), (width // seq, width)], rest
    )
    output = in_order(output)
    s_bq, s_bv, s_ga, s_sa, s_bo, s_gf, s_sf, s_bd, s_b_up = (
        v.reshape(-1) for v in vec
    )
    return (
        output, d_tokens, s_qkv, s_bq, s_bv, s_out, s_bo, s_ga, s_sa, s_up, s_b_up, s_down, s_bd,
        s_gf, s_sf,
    )


def solution(mesh):
    dp, seq = mesh.shape["dp"], mesh.shape["seq"]
    rows = P("dp", "seq", None)
    placed = (rows, P("dp")) + (P(),) * 14 + (rows,)
    cut, line = P("seq", None), P("seq")

    def body(*args):
        return local(dp, seq, *args)

    return jax.shard_map(
        body,
        mesh=mesh,
        in_specs=placed,
        out_specs=(
            rows, rows, cut, line, line, cut, line, line, line, cut, line, cut, line, line, line,
        ),
        check_vma=False,
    )
```
